256 devices in a mesh: gr: 16 (over x, y_hi, core), gc: 16 (over y_lo, z).
Axes of the slice: x: 4, y: 4 (y_hi: 2, y_lo: 2; y = y_hi * 2 + y_lo), z: 8, core: 2. Of those that a mesh axis runs over, the one named last changes fastest.
Arguments:
- border: bfloat16 [96, 768, 2048], P('gc', None, 'gr'), may hold values from -1 to 1
- row_scale: float32 [96, 768], P('gc'), may hold values from 0.1 to 10
- block_pick: int32 [96, 16], replicated, may hold values from 0 to 3
- given_diag: float32 [8192], replicated, may hold values from 0.5 to 4
Outputs:
- factored: float32 [8192, 8192], P('gr', 'gc')
The draws below stay inside these ranges and needn't reach their ends.
All inputs are finite; a program needn't handle non-finite values.
Results may differ from the reference program's by a relative error of at most 0.00097.
Values may be sent and summed in bfloat16 or wider, within the bound.
No kernel may reach another device: no remote copies, remote signals or barrier semaphores. Data moves between devices by JAX's collectives and lax.ppermute only.
A program may use at most 128 MiB of HBM per device.

```python
import math
import jax
import jax.numpy as jnp
from jax import lax

N = 8192
BLK = 128
NWIN = 16
WSPAN = 4
R = 768
PW = 256
PANELS = 2
SCEN = 96


def draw_border(key, part):
    keys = jax.random.split(jax.random.fold_in(key, 17), 3)
    width = NWIN * BLK
    spread = (R * SCEN / WSPAN) ** (-0.5)
    noise = jnp.clip(jax.random.normal(keys[0], (SCEN, R, width), jnp.float32), -4.0, 4.0)
    loads = jnp.clip(jax.random.normal(keys[1], (SCEN, R, 3), jnp.float32), -3.0, 3.0)
    factors = jnp.clip(jax.random.normal(keys[2], (SCEN, 3, width), jnp.float32), -3.0, 3.0)
    lowpart = loads[:, :, 0:1] * factors[:, 0:1, :]
    lowpart = lowpart + loads[:, :, 1:2] * factors[:, 1:2, :]
    lowpart = lowpart + loads[:, :, 2:3] * factors[:, 2:3, :]
    values = jnp.clip(spread * (noise + 0.5 * lowpart), -1.0, 1.0)
    return values.astype(jnp.bfloat16)


def touch_ends(entries, stream_key, least, high):
    extent = entries.shape
    spot = [jax.random.randint(jax.random.fold_in(stream_key, axis), (), 0, extent[axis]) for axis in range(len(extent))]
    entries = entries.at[tuple(spot)].set(least)
    longest = extent.index(max(extent))
    spot[longest] = (spot[longest] + 1) % extent[longest]
    return entries.at[tuple(spot)].set(high)


def block_levels(key, extent, cuts, low, high):
    def one(position, parts):
        steps = jax.random.uniform(jax.random.fold_in(jax.random.fold_in(key, 6), position), (parts,), jnp.float32, low / len(cuts), high / len(cuts))
        return jnp.repeat(jnp.exp(steps), extent[position] // parts).reshape((-1,) + (1,) * (len(extent) - position - 1))

    loudness = one(*cuts[0])
    for cut in cuts[1:]:
        loudness = loudness * one(*cut)
    return loudness


def setup_inputs(seed: int = 0) -> dict:
    key_list = jax.random.split(jax.random.key(seed), 5)
    border = draw_border(jax.random.fold_in(key_list[4], 71), 0)
    row_scale = jnp.clip(jnp.exp(math.log(10.0) - 4.6051702 * jax.random.uniform(key_list[1], (SCEN, R), jnp.float32) ** block_levels(key_list[1], (SCEN, R), ((0, 16),), -0.2, 0.2)), 0.1, 10.0)
    block_pick = touch_ends(jax.random.randint(key_list[2], (SCEN, NWIN), 0, WSPAN), jax.random.fold_in(key_list[2], 1), 0, WSPAN - 1).astype(jnp.int32)
    given_diag = jnp.clip(jnp.exp(jax.random.uniform(key_list[3], (N,), jnp.float32, math.log(0.5), math.log(4.0))), 0.5, 4.0)
    return {"border": border, "row_scale": row_scale, "block_pick": block_pick, "given_diag": given_diag}


def reference(border, row_scale, block_pick, given_diag):
    window_base = jnp.arange(NWIN, dtype=jnp.int32) * WSPAN
    within = jnp.arange(BLK, dtype=jnp.int32)

    def add_scenario(total, item):
        slab, scale_row, pick_row = item
        scaled = (jnp.sqrt(scale_row)[:, None] * slab.astype(jnp.float32)).astype(jnp.bfloat16)
        wide = scaled.astype(jnp.float32)
        gram = jnp.dot(wide.T.astype(jnp.float32), wide.astype(jnp.float32), precision=lax.Precision.HIGHEST, preferred_element_type=jnp.float32)
        blocks = window_base + pick_row.astype(jnp.int32)
        columns = (blocks[:, None] * BLK + within[None, :]).reshape(-1).astype(jnp.int32)
        total = total.at[columns[:, None], columns[None, :]].add(gram)
        return (total, None)
    start = jnp.diag(given_diag.astype(jnp.float32))
    factored, _ = lax.scan(add_scenario, start, (border, row_scale, block_pick))
    row_global = jnp.arange(N, dtype=jnp.int32)
    for panel_index in range(PANELS):
        first_col = panel_index * PW
        past_col = first_col + PW
        chol_block = jnp.linalg.cholesky(factored[first_col:past_col, first_col:past_col])
        column_part = factored[:, first_col:past_col]
        solved = jax.scipy.linalg.solve_triangular(chol_block, column_part.T, lower=True).T
        solved = jnp.where((row_global >= past_col)[:, None], solved, 0.0)
        solved = solved.at[first_col:past_col].set(chol_block)
        product = jnp.dot(solved.astype(jnp.float32), solved.T.astype(jnp.float32), precision=lax.Precision.HIGHEST, preferred_element_type=jnp.float32)
        trailing = (row_global >= past_col)[:, None] & (row_global >= past_col)[None, :]
        factored = jnp.where(trailing, factored - product, factored)
        factored = factored.at[:, first_col:past_col].set(solved)
        factored = factored.at[first_col:past_col, past_col:].set(0.0)
    return factored
```

```python
import jax
import jax.numpy as jnp
import numpy as np
from jax import lax
from jax.experimental import pallas as pl
from jax.experimental.pallas import tpu as pltpu
from jax.sharding import Mesh, PartitionSpec as P

N = 8192
BLK = 128
NWIN = 16
SPAN = 4
R = 768
GROUP = 6
HALF = 3
SLICE = 8
ROWS = HALF * BLK + GROUP * SLICE

AXES = ("x", "yh", "core", "yl", "z")
SIZES = (4, 2, 2, 2, 8)
GR = ("x", "yh", "core")
GC = ("yl", "z")
HIGH = lax.Precision.HIGHEST
CONTRACT_ROWS = (((0,), (0,)), ((), ()))
CONTRACT_COLS = (((1,), (1,)), ((), ()))


def gram_kernel(meta, first, mine, same, other, lead, out):
    q = pl.program_id(0)
    c = meta[1]
    at_same = 2 * q + c
    at_other = 2 * q + 1 - c
    for k in range(HALF):
        pair = jnp.concatenate([same[0, k], other[0, k]], axis=1)
        tiles = lax.dot_general(
            mine[k], pair, CONTRACT_ROWS, preferred_element_type=jnp.float32
        )
        out[at_same, k * BLK : (k + 1) * BLK, :] = tiles[:, :BLK]
        out[at_other, k * BLK : (k + 1) * BLK, :] = tiles[:, BLK:]

    @pl.when(q == 0)
    def _():
        for m in range(GROUP):
            if m < HALF:
                tile = lax.dot_general(
                    first[m], lead[m], CONTRACT_ROWS, preferred_element_type=jnp.float32
                )
            else:
                tile = out[0, (m - HALF) * BLK : (m - HALF + 1) * BLK, :]
            base = HALF * BLK + m * SLICE
            for j in range(NWIN):
                out[j, base : base + SLICE, :] = tile[j * SLICE : (j + 1) * SLICE, :]


def gram_slots(meta, scaled, same, other, lead):
    def pick_half(q, meta):
        return (jnp.where((q > meta[0]) | ((q == meta[0]) & (meta[1] == 0)), 0, 1), 0, 0)

    whole = (HALF, R, BLK)
    grid_spec = pltpu.PrefetchScalarGridSpec(
        num_scalar_prefetch=1,
        grid=(NWIN // 2,),
        in_specs=[
            pl.BlockSpec(whole, lambda q, meta: (0, 0, 0)),
            pl.BlockSpec(whole, pick_half),
            pl.BlockSpec((1,) + whole, lambda q, meta: (q, 0, 0, 0)),
            pl.BlockSpec((1,) + whole, lambda q, meta: (q, 0, 0, 0)),
            pl.BlockSpec(whole, lambda q, meta: (0, 0, 0)),
        ],
        out_specs=pl.BlockSpec((NWIN, ROWS, BLK), lambda q, meta: (0, 0, 0)),
    )
    return pl.pallas_call(
        gram_kernel,
        grid_spec=grid_spec,
        out_shape=jax.ShapeDtypeStruct((NWIN, ROWS, BLK), jnp.float32),
        name="gram_slots",
    )(meta, scaled, scaled, same, other, lead)


def place_kernel(meta, picks, slots, inverse, part, solved, panel):
    g = pl.program_id(0)
    i = meta[2]
    j = meta[3]

    @pl.when(g == 0)
    def _():
        part[...] = jnp.zeros_like(part)
        panel[...] = jnp.zeros_like(panel)

    base = g * GROUP + jnp.where(i < j, 0, HALF)
    for k in range(HALF):
        a = picks[base + k, i]
        b = picks[base + k, j]
        part[a, b] += slots[0, k * BLK : (k + 1) * BLK, :]
    for m in range(GROUP):
        a = picks[g * GROUP + m, i]
        b = picks[g * GROUP + m, 0]
        start = HALF * BLK + m * SLICE
        panel[b, a] += slots[0, start : start + SLICE, :]

    @pl.when(g == pl.num_programs(0) - 1)
    def _():
        for b in range(SPAN):
            rows = panel[b].reshape(SPAN * SLICE, BLK)
            done = lax.dot_general(
                rows,
                inverse[b],
                CONTRACT_COLS,
                precision=HIGH,
                preferred_element_type=jnp.float32,
            )
            solved[b] = done.reshape(SPAN, SLICE, BLK)


def place(meta, picks, slots, inverse):
    grid_spec = pltpu.PrefetchScalarGridSpec(
        num_scalar_prefetch=2,
        grid=(NWIN,),
        in_specs=[
            pl.BlockSpec((1, ROWS, BLK), lambda g, *_: (g, 0, 0)),
            pl.BlockSpec((SPAN, BLK, BLK), lambda g, *_: (0, 0, 0)),
        ],
        out_specs=[
            pl.BlockSpec((SPAN, SPAN, BLK, BLK), lambda g, *_: (0, 0, 0, 0)),
            pl.BlockSpec((SPAN, SPAN, SLICE, BLK), lambda g, *_: (0, 0, 0, 0)),
        ],
        scratch_shapes=[pltpu.VMEM((SPAN, SPAN, SLICE, BLK), jnp.float32)],
    )
    return pl.pallas_call(
        place_kernel,
        grid_spec=grid_spec,
        out_shape=[
            jax.ShapeDtypeStruct((SPAN, SPAN, BLK, BLK), jnp.float32),
            jax.ShapeDtypeStruct((SPAN, SPAN, SLICE, BLK), jnp.float32),
        ],
        name="place_tiles",
    )(meta, picks, slots, inverse)


def finish_kernel(meta, part, mirror, left, right, diag, chol, out):
    i = meta[2]
    j = meta[3]

    def block_rows(ref, a):
        return jnp.concatenate([ref[:, b, a].reshape(BLK, BLK) for b in range(SPAN)], axis=1)

    lefts = [block_rows(left, a) for a in range(SPAN)]
    inside = (i > 0) & (j > 0)

    @pl.when(inside & (i != j))
    def _():
        for a in range(SPAN):
            for b in range(SPAN):
                out[a * BLK : (a + 1) * BLK, b * BLK : (b + 1) * BLK] = part[a, b] + mirror[b, a].T

    @pl.when(inside & (i == j))
    def _():
        out[...] = jnp.zeros_like(out)
        for a in range(SPAN):
            out[a * BLK : (a + 1) * BLK, a * BLK : (a + 1) * BLK] = diag[a]

    @pl.when(inside)
    def _():
        for b in range(SPAN):
            rights = block_rows(right, b)
            for a in range(SPAN):
                spot = (slice(a * BLK, (a + 1) * BLK), slice(b * BLK, (b + 1) * BLK))
                out[spot] = out[spot] - lax.dot_general(
                    lefts[a],
                    rights,
                    CONTRACT_COLS,
                    precision=HIGH,
                    preferred_element_type=jnp.float32,
                )

    @pl.when((i == 0))
    def _():
        out[...] = jnp.zeros_like(out)

    @pl.when((i == 0) & (j == 0))
    def _():
        for a in range(SPAN):
            out[a * BLK : (a + 1) * BLK, a * BLK : (a + 1) * BLK] = chol[a]

    @pl.when((i > 0) & (j == 0))
    def _():
        for a in range(SPAN):
            out[a * BLK : (a + 1) * BLK, :] = lefts[a]


def finish(meta, part, mirror, left, right, diag, chol):
    def full(shape):
        zeros = (0,) * len(shape)
        return pl.BlockSpec(shape, lambda t, meta: zeros)

    blocks = (SPAN, SPAN, BLK, BLK)
    slices = (NWIN, SPAN, SPAN, SLICE, BLK)
    small = (SPAN, BLK, BLK)
    size = (SPAN * BLK, SPAN * BLK)
    grid_spec = pltpu.PrefetchScalarGridSpec(
        num_scalar_prefetch=1,
        grid=(1,),
        in_specs=[full(s) for s in (blocks, blocks, slices, slices, small, small)],
        out_specs=full(size),
    )
    return pl.pallas_call(
        finish_kernel,
        grid_spec=grid_spec,
        out_shape=jax.ShapeDtypeStruct(size, jnp.float32),
        name="finish",
    )(meta, part, mirror, left, right, diag, chol)


def swap_pairs(size, bit):
    return [(k, k ^ bit) for k in range(size)]


def spread_rows(v, steps):
    for step in steps:
        if step == "core":
            v = v + lax.ppermute(v, "core", [(0, 1)])
        elif step == "yh":
            v = v + lax.ppermute(v, "yh", [(0, 1)])
        else:
            up = lax.ppermute(v, "x", [(0, 1)])
            down = lax.ppermute(v, "x", [(0, 3)])
            v = v + up + down
            v = v + lax.ppermute(v, "x", [(1, 2)])
    return v


def body(border, row_scale, block_pick, given_diag):
    i = lax.axis_index(GR).astype(jnp.int32)
    j = lax.axis_index(GC).astype(jnp.int32)
    chip = i // 2
    core = i % 2
    meta = jnp.stack([chip, core, i, j])

    scaled = (jnp.sqrt(row_scale)[:, :, None] * border.astype(jnp.float32)).astype(jnp.bfloat16)

    peers = jnp.arange(8, dtype=jnp.int32)
    early = (peers < chip) | ((peers == chip) & (core == 1))
    slots = jnp.where(early[:, None, None, None], scaled[None, :HALF], scaled[None, HALF:])
    same = lax.all_to_all(slots, ("x", "yh"), 0, 0, tiled=True)
    other = lax.ppermute(same, "core", [(0, 1), (1, 0)])

    lead = spread_rows(
        jnp.where(i == 0, scaled[:HALF], jnp.zeros_like(scaled[:HALF])), ("yh", "x", "core")
    )

    own = jnp.einsum("srx,sry->sxy", scaled, scaled, preferred_element_type=jnp.float32)
    own_pick = lax.dynamic_slice(block_pick, (j * GROUP, i), (GROUP, 1))[:, 0]
    hot = own_pick[:, None] == jnp.arange(SPAN, dtype=jnp.int32)[None, :]
    diag = jnp.sum(jnp.where(hot[:, :, None, None], own[:, None], 0.0), axis=0)
    for bit in (1, 2, 4):
        diag = diag + lax.ppermute(diag, "z", swap_pairs(8, bit))
    diag = diag + lax.ppermute(diag, "yl", swap_pairs(2, 1))
    eye = jnp.eye(BLK, dtype=jnp.float32)
    given_here = lax.dynamic_slice(given_diag, (i * SPAN * BLK,), (SPAN * BLK,))
    diag = diag + given_here.reshape(SPAN, 1, BLK) * eye
    corner = spread_rows(jnp.where(i == 0, diag, 0.0), ("core", "yh", "x"))
    chol = jnp.linalg.cholesky(corner)
    inverse = lax.linalg.triangular_solve(
        chol, jnp.broadcast_to(eye, chol.shape), left_side=True, lower=True
    )

    tiles = gram_slots(meta, scaled, same, other, lead)
    tiles = lax.all_to_all(tiles, GC, 0, 0, tiled=True)
    part, solved = place(meta, block_pick, tiles, inverse)
    everywhere = [(r * NWIN + c, c * NWIN + r) for r in range(NWIN) for c in range(NWIN)]
    turned = lax.ppermute(solved, AXES, everywhere)
    mirror = lax.ppermute(part, AXES, everywhere)
    copies = (NWIN,) + solved.shape
    left = lax.all_to_all(jnp.broadcast_to(solved, copies), GC, 0, 0, tiled=True)
    right = lax.all_to_all(jnp.broadcast_to(turned, copies), GR, 0, 0, tiled=True)
    return finish(meta, part, mirror, left, right, diag, chol)


def solution(mesh):
    fine = Mesh(np.asarray(mesh.devices).reshape(SIZES), AXES)
    in_specs = (P(GC, None, GR), P(GC, None), P(), P())
    return jax.shard_map(
        body, mesh=fine, in_specs=in_specs, out_specs=P(GR, GC), check_vma=False
    )
```

```python
import jax
import jax.numpy as jnp
import numpy as np
from jax import lax
from jax.experimental import pallas as pl
from jax.experimental.pallas import tpu as pltpu
from jax.sharding import Mesh, PartitionSpec as P

BLK = 128
NWIN = 16
SPAN = 4
R = 768
GROUP = 6
HALF = 3
SLICE = 8
ROWS = HALF * BLK + GROUP * SLICE
PLACE = 4

AXES = ("x", "yh", "core", "yl", "z")
SIZES = (4, 2, 2, 2, 8)
GR = ("x", "yh", "core")
GC = ("yl", "z")
HIGH = lax.Precision.HIGHEST
CONTRACT_ROWS = (((0,), (0,)), ((), ()))
CONTRACT_COLS = (((1,), (1,)), ((), ()))


def gram_kernel(meta, mine, same, other, out, late):
    q = pl.program_id(0)
    c = meta[1]
    at_same = 2 * q + c
    at_other = 2 * q + 1 - c
    for k in range(HALF):
        pair = jnp.concatenate([same[0, k], other[0, k]], axis=1)
        tiles = lax.dot_general(
            mine[k], pair, CONTRACT_ROWS, preferred_element_type=jnp.float32
        )
        out[at_same, k * BLK : (k + 1) * BLK, :] = tiles[:, :BLK]
        out[at_other, k * BLK : (k + 1) * BLK, :] = tiles[:, BLK:]

    @pl.when(q == 0)
    def _():
        late[...] = out[0, : HALF * BLK, :].reshape(HALF, BLK, BLK)
        out[:, HALF * BLK :, :] = jnp.zeros((NWIN, GROUP * SLICE, BLK), jnp.float32)


def gram_slots(meta, scaled, same, other):
    def pick_half(q, meta):
        return (jnp.where((q > meta[0]) | ((q == meta[0]) & (meta[1] == 0)), 0, 1), 0, 0)

    whole = (HALF, R, BLK)
    grid_spec = pltpu.PrefetchScalarGridSpec(
        num_scalar_prefetch=1,
        grid=(NWIN // 2,),
        in_specs=[
            pl.BlockSpec(whole, pick_half),
            pl.BlockSpec((1,) + whole, lambda q, meta: (q, 0, 0, 0)),
            pl.BlockSpec((1,) + whole, lambda q, meta: (q, 0, 0, 0)),
        ],
        out_specs=[
            pl.BlockSpec((NWIN, ROWS, BLK), lambda q, meta: (0, 0, 0)),
            pl.BlockSpec((HALF, BLK, BLK), lambda q, meta: (0, 0, 0)),
        ],
    )
    return pl.pallas_call(
        gram_kernel,
        grid_spec=grid_spec,
        out_shape=[
            jax.ShapeDtypeStruct((NWIN, ROWS, BLK), jnp.float32),
            jax.ShapeDtypeStruct((HALF, BLK, BLK), jnp.float32),
        ],
        name="gram_slots",
    )(meta, scaled, same, other)


def panel_kernel(first, lead, late, held, out):
    del held
    for m in range(GROUP):
        if m < HALF:
            tile = lax.dot_general(
                first[m], lead[m], CONTRACT_ROWS, preferred_element_type=jnp.float32
            )
        else:
            tile = late[m - HALF]
        for j in range(NWIN):
            out[j, m * SLICE : (m + 1) * SLICE, :] = tile[j * SLICE : (j + 1) * SLICE, :]


def panel_slots(scaled, lead, late, slots):
    whole = (HALF, R, BLK)
    rows = GROUP * SLICE
    return pl.pallas_call(
        panel_kernel,
        grid=(1,),
        in_specs=[
            pl.BlockSpec(whole, lambda t: (0, 0, 0)),
            pl.BlockSpec(whole, lambda t: (0, 0, 0)),
            pl.BlockSpec((HALF, BLK, BLK), lambda t: (0, 0, 0)),
            pl.BlockSpec(memory_space=pl.ANY),
        ],
        out_specs=pl.BlockSpec((NWIN, rows, BLK), lambda t: (0, HALF * BLK // rows, 0)),
        out_shape=jax.ShapeDtypeStruct(slots.shape, slots.dtype),
        input_output_aliases={3: 0},
        name="panel_slots",
    )(scaled, lead, late, slots)


def place_kernel(meta, picks, slots, part, panel):
    g = pl.program_id(0)
    i = meta[2]
    j = meta[3]

    @pl.when(g == 0)
    def _():
        part[...] = jnp.zeros_like(part)
        panel[...] = jnp.zeros_like(panel)

    for u in range(PLACE):
        group = g * PLACE + u
        base = group * GROUP + jnp.where(i < j, 0, HALF)
        for k in range(HALF):
            a = picks[base + k, i]
            b = picks[base + k, j]
            part[a, b] += slots[u, k * BLK : (k + 1) * BLK, :]
        for m in range(GROUP):
            a = picks[group * GROUP + m, i]
            b = picks[group * GROUP + m, 0]
            start = HALF * BLK + m * SLICE
            panel[b, a] += slots[u, start : start + SLICE, :]


def place(meta, picks, slots):
    grid_spec = pltpu.PrefetchScalarGridSpec(
        num_scalar_prefetch=2,
        grid=(NWIN // PLACE,),
        in_specs=[pl.BlockSpec((PLACE, ROWS, BLK), lambda g, *_: (g, 0, 0))],
        out_specs=[
            pl.BlockSpec((SPAN, SPAN, BLK, BLK), lambda g, *_: (0, 0, 0, 0)),
            pl.BlockSpec((SPAN, SPAN, SLICE, BLK), lambda g, *_: (0, 0, 0, 0)),
        ],
    )
    return pl.pallas_call(
        place_kernel,
        grid_spec=grid_spec,
        out_shape=[
            jax.ShapeDtypeStruct((SPAN, SPAN, BLK, BLK), jnp.float32),
            jax.ShapeDtypeStruct((SPAN, SPAN, SLICE, BLK), jnp.float32),
        ],
        name="place_tiles",
    )(meta, picks, slots)


def finish_kernel(meta, part, mirror, left, right, diag, chol, inverse, out):
    i = meta[2]
    j = meta[3]

    def block_rows(ref, a):
        solved = [
            lax.dot_general(
                ref[:, b, a].reshape(BLK, BLK),
                inverse[b],
                CONTRACT_COLS,
                precision=HIGH,
                preferred_element_type=jnp.float32,
            )
            for b in range(SPAN)
        ]
        return jnp.concatenate(solved, axis=1)

    lefts = [block_rows(left, a) for a in range(SPAN)]
    inside = (i > 0) & (j > 0)

    @pl.when(inside & (i != j))
    def _():
        for a in range(SPAN):
            for b in range(SPAN):
                out[a * BLK : (a + 1) * BLK, b * BLK : (b + 1) * BLK] = part[a, b] + mirror[b, a].T

    @pl.when(inside & (i == j))
    def _():
        out[...] = jnp.zeros_like(out)
        for a in range(SPAN):
            out[a * BLK : (a + 1) * BLK, a * BLK : (a + 1) * BLK] = diag[a]

    @pl.when(inside)
    def _():
        for b in range(SPAN):
            rights = block_rows(right, b)
            for a in range(SPAN):
                spot = (slice(a * BLK, (a + 1) * BLK), slice(b * BLK, (b + 1) * BLK))
                out[spot] = out[spot] - lax.dot_general(
                    lefts[a],
                    rights,
                    CONTRACT_COLS,
                    precision=HIGH,
                    preferred_element_type=jnp.float32,
                )

    @pl.when((i == 0))
    def _():
        out[...] = jnp.zeros_like(out)

    @pl.when((i == 0) & (j == 0))
    def _():
        for a in range(SPAN):
            out[a * BLK : (a + 1) * BLK, a * BLK : (a + 1) * BLK] = chol[a]

    @pl.when((i > 0) & (j == 0))
    def _():
        for a in range(SPAN):
            out[a * BLK : (a + 1) * BLK, :] = lefts[a]


def finish(meta, part, mirror, left, right, diag, chol, inverse):
    def full(shape):
        zeros = (0,) * len(shape)
        return pl.BlockSpec(shape, lambda t, meta: zeros)

    blocks = (SPAN, SPAN, BLK, BLK)
    slices = (NWIN, SPAN, SPAN, SLICE, BLK)
    small = (SPAN, BLK, BLK)
    size = (SPAN * BLK, SPAN * BLK)
    grid_spec = pltpu.PrefetchScalarGridSpec(
        num_scalar_prefetch=1,
        grid=(1,),
        in_specs=[full(s) for s in (blocks, blocks, slices, slices, small, small, small)],
        out_specs=full(size),
    )
    return pl.pallas_call(
        finish_kernel,
        grid_spec=grid_spec,
        out_shape=jax.ShapeDtypeStruct(size, jnp.float32),
        name="finish",
    )(meta, part, mirror, left, right, diag, chol, inverse)


def swap_pairs(size, bit):
    return [(k, k ^ bit) for k in range(size)]


def spread_rows(v, steps):
    for step in steps:
        if step == "core":
            v = v + lax.ppermute(v, "core", [(0, 1)])
        elif step == "yh":
            v = v + lax.ppermute(v, "yh", [(0, 1)])
        else:
            up = lax.ppermute(v, "x", [(0, 1)])
            down = lax.ppermute(v, "x", [(0, 3)])
            v = v + up + down
            v = v + lax.ppermute(v, "x", [(1, 2)])
    return v


def body(border, row_scale, block_pick, given_diag):
    i = lax.axis_index(GR).astype(jnp.int32)
    j = lax.axis_index(GC).astype(jnp.int32)
    chip = i // 2
    core = i % 2
    meta = jnp.stack([chip, core, i, j])

    scaled = (jnp.sqrt(row_scale)[:, :, None] * border.astype(jnp.float32)).astype(jnp.bfloat16)

    own = jnp.einsum("srx,sry->sxy", scaled, scaled, preferred_element_type=jnp.float32)
    own_pick = lax.dynamic_slice(block_pick, (j * GROUP, i), (GROUP, 1))[:, 0]
    hot = own_pick[:, None] == jnp.arange(SPAN, dtype=jnp.int32)[None, :]
    diag = jnp.sum(jnp.where(hot[:, :, None, None], own[:, None], 0.0), axis=0)
    for bit in (1, 2, 4):
        diag = diag + lax.ppermute(diag, "z", swap_pairs(8, bit))

    peers = jnp.arange(8, dtype=jnp.int32)
    early = (peers < chip) | ((peers == chip) & (core == 1))
    slots = jnp.where(early[:, None, None, None], scaled[None, :HALF], scaled[None, HALF:])
    same = lax.all_to_all(slots, ("x", "yh"), 0, 0, tiled=True)
    same, diag = lax.optimization_barrier((same, diag))
    other = lax.ppermute(same, "core", [(0, 1), (1, 0)])

    cut = R // 2
    rootly = jnp.where(i == 0, scaled[:HALF], jnp.zeros_like(scaled[:HALF]))
    piece = rootly[:, :cut] + lax.ppermute(rootly[:, cut:], "core", [(0, 1)])
    piece = spread_rows(piece, ("yh", "x"))
    tiles, late = gram_slots(meta, scaled, same, other)
    piece, late = lax.optimization_barrier((piece, late))
    twin = lax.ppermute(piece, "core", [(0, 1), (1, 0)])
    lead = jnp.concatenate(
        [jnp.where(core == 0, piece, twin), jnp.where(core == 0, twin, piece)], axis=1
    )

    diag = diag + lax.ppermute(diag, "yl", swap_pairs(2, 1))
    eye = jnp.eye(BLK, dtype=jnp.float32)
    given_here = lax.dynamic_slice(given_diag, (i * SPAN * BLK,), (SPAN * BLK,))
    diag = diag + given_here.reshape(SPAN, 1, BLK) * eye
    corner = spread_rows(jnp.where(i == 0, diag, 0.0), ("core", "x", "yh"))

    tiles = panel_slots(scaled, lead, late, tiles)
    tiles, corner = lax.optimization_barrier((tiles, corner))
    tiles = lax.all_to_all(tiles, GC, 0, 0, tiled=True)
    chol = jnp.linalg.cholesky(corner)
    tiles, chol = lax.optimization_barrier((tiles, chol))
    inverse = lax.linalg.triangular_solve(
        chol, jnp.broadcast_to(eye, chol.shape), left_side=True, lower=True
    )

    part, strip = place(meta, block_pick, tiles)
    everywhere = [(r * NWIN + c, c * NWIN + r) for r in range(NWIN) for c in range(NWIN)]
    copies = (NWIN,) + strip.shape
    turned = lax.ppermute(strip, AXES, everywhere)
    mirror = lax.ppermute(part, AXES, everywhere)
    left = lax.all_to_all(jnp.broadcast_to(strip, copies), GC, 0, 0, tiled=True)
    right = lax.all_to_all(jnp.broadcast_to(turned, copies), GR, 0, 0, tiled=True)
    return finish(meta, part, mirror, left, right, diag, chol, inverse)


def solution(mesh):
    fine = Mesh(np.asarray(mesh.devices).reshape(SIZES), AXES)
    in_specs = (P(GC, None, GR), P(GC, None), P(), P())
    return jax.shard_map(body, mesh=fine, in_specs=in_specs, out_specs=P(GR, GC), check_vma=False)
```

```python
import jax
import jax.numpy as jnp
import numpy as np
from jax import lax
from jax.experimental import pallas as pl
from jax.experimental.pallas import tpu as pltpu
from jax.sharding import Mesh, PartitionSpec as P

BLK = 128
NWIN = 16
SPAN = 4
R = 768
GROUP = 6
HALF = 3
SLICE = 8
ROWS = HALF * BLK
PLACE = 4

AXES = ("x", "yh", "core", "yl", "z")
SIZES = (4, 2, 2, 2, 8)
GR = ("x", "yh", "core")
GC = ("yl", "z")
HIGH = lax.Precision.HIGHEST
CONTRACT_ROWS = (((0,), (0,)), ((), ()))
CONTRACT_COLS = (((1,), (1,)), ((), ()))


def gram_kernel(meta, mine, same, other, out, late):
    q = pl.program_id(0)
    c = meta[1]
    at_same = 2 * q + c
    at_other = 2 * q + 1 - c
    for k in range(HALF):
        pair = jnp.concatenate([same[0, k], other[0, k]], axis=1)
        tiles = lax.dot_general(
            mine[k], pair, CONTRACT_ROWS, preferred_element_type=jnp.float32
        )
        out[at_same, k * BLK : (k + 1) * BLK, :] = tiles[:, :BLK]
        out[at_other, k * BLK : (k + 1) * BLK, :] = tiles[:, BLK:]

    @pl.when(q == 0)
    def _():
        late[...] = out[0].reshape(HALF, BLK, BLK)


def gram_slots(meta, scaled, same, other):
    def pick_half(q, meta):
        return (jnp.where((q > meta[0]) | ((q == meta[0]) & (meta[1] == 0)), 0, 1), 0, 0)

    whole = (HALF, R, BLK)
    grid_spec = pltpu.PrefetchScalarGridSpec(
        num_scalar_prefetch=1,
        grid=(NWIN // 2,),
        in_specs=[
            pl.BlockSpec(whole, pick_half),
            pl.BlockSpec((1,) + whole, lambda q, meta: (q, 0, 0, 0)),
            pl.BlockSpec((1,) + whole, lambda q, meta: (q, 0, 0, 0)),
        ],
        out_specs=[
            pl.BlockSpec((NWIN, ROWS, BLK), lambda q, meta: (0, 0, 0)),
            pl.BlockSpec((HALF, BLK, BLK), lambda q, meta: (0, 0, 0)),
        ],
    )
    return pl.pallas_call(
        gram_kernel,
        grid_spec=grid_spec,
        out_shape=[
            jax.ShapeDtypeStruct((NWIN, ROWS, BLK), jnp.float32),
            jax.ShapeDtypeStruct((HALF, BLK, BLK), jnp.float32),
        ],
        name="gram_slots",
    )(meta, scaled, same, other)


def panel_kernel(first, lead, late, out):
    for m in range(GROUP):
        if m < HALF:
            tile = lax.dot_general(
                first[m], lead[m], CONTRACT_ROWS, preferred_element_type=jnp.float32
            )
        else:
            tile = late[m - HALF]
        for j in range(NWIN):
            out[j, m * SLICE : (m + 1) * SLICE, :] = tile[j * SLICE : (j + 1) * SLICE, :]


def panel_slots(scaled, lead, late):
    whole = (HALF, R, BLK)
    shape = (NWIN, GROUP * SLICE, BLK)
    return pl.pallas_call(
        panel_kernel,
        grid=(1,),
        in_specs=[
            pl.BlockSpec(whole, lambda t: (0, 0, 0)),
            pl.BlockSpec(whole, lambda t: (0, 0, 0)),
            pl.BlockSpec((HALF, BLK, BLK), lambda t: (0, 0, 0)),
        ],
        out_specs=pl.BlockSpec(shape, lambda t: (0, 0, 0)),
        out_shape=jax.ShapeDtypeStruct(shape, jnp.float32),
        name="panel_slots",
    )(scaled, lead, late)


def place_kernel(meta, picks, slots, part):
    g = pl.program_id(0)
    i = meta[2]
    j = meta[3]

    @pl.when(g == 0)
    def _():
        part[...] = jnp.zeros_like(part)

    for u in range(PLACE):
        base = (g * PLACE + u) * GROUP + jnp.where(i < j, 0, HALF)
        for k in range(HALF):
            a = picks[base + k, i]
            b = picks[base + k, j]
            part[a, b] += slots[u, k * BLK : (k + 1) * BLK, :]


def place(meta, picks, slots):
    grid_spec = pltpu.PrefetchScalarGridSpec(
        num_scalar_prefetch=2,
        grid=(NWIN // PLACE,),
        in_specs=[pl.BlockSpec((PLACE, ROWS, BLK), lambda g, *_: (g, 0, 0))],
        out_specs=pl.BlockSpec((SPAN, SPAN, BLK, BLK), lambda g, *_: (0, 0, 0, 0)),
    )
    return pl.pallas_call(
        place_kernel,
        grid_spec=grid_spec,
        out_shape=jax.ShapeDtypeStruct((SPAN, SPAN, BLK, BLK), jnp.float32),
        name="place_tiles",
    )(meta, picks, slots)


def strip_kernel(meta, picks, slots, strip):
    i = meta[2]
    strip[...] = jnp.zeros_like(strip)
    for g in range(NWIN):
        for m in range(GROUP):
            a = picks[g * GROUP + m, i]
            b = picks[g * GROUP + m, 0]
            strip[b, a] += slots[g, m * SLICE : (m + 1) * SLICE, :]


def place_strip(meta, picks, slots):
    shape = (SPAN, SPAN, SLICE, BLK)
    grid_spec = pltpu.PrefetchScalarGridSpec(
        num_scalar_prefetch=2,
        grid=(1,),
        in_specs=[pl.BlockSpec(slots.shape, lambda t, *_: (0, 0, 0))],
        out_specs=pl.BlockSpec(shape, lambda t, *_: (0, 0, 0, 0)),
    )
    return pl.pallas_call(
        strip_kernel,
        grid_spec=grid_spec,
        out_shape=jax.ShapeDtypeStruct(shape, jnp.float32),
        name="place_strip",
    )(meta, picks, slots)


def finish_kernel(meta, part, mirror, left, right, diag, chol, inverse, out):
    i = meta[2]
    j = meta[3]

    def block_rows(ref, a):
        solved = [
            lax.dot_general(
                ref[:, b, a].reshape(BLK, BLK),
                inverse[b],
                CONTRACT_COLS,
                precision=HIGH,
                preferred_element_type=jnp.float32,
            )
            for b in range(SPAN)
        ]
        return jnp.concatenate(solved, axis=1)

    lefts = [block_rows(left, a) for a in range(SPAN)]
    inside = (i > 0) & (j > 0)

    @pl.when(inside & (i != j))
    def _():
        for a in range(SPAN):
            for b in range(SPAN):
                out[a * BLK : (a + 1) * BLK, b * BLK : (b + 1) * BLK] = part[a, b] + mirror[b, a].T

    @pl.when(inside & (i == j))
    def _():
        out[...] = jnp.zeros_like(out)
        for a in range(SPAN):
            out[a * BLK : (a + 1) * BLK, a * BLK : (a + 1) * BLK] = diag[a]

    @pl.when(inside)
    def _():
        for b in range(SPAN):
            rights = block_rows(right, b)
            for a in range(SPAN):
                spot = (slice(a * BLK, (a + 1) * BLK), slice(b * BLK, (b + 1) * BLK))
                out[spot] = out[spot] - lax.dot_general(
                    lefts[a],
                    rights,
                    CONTRACT_COLS,
                    precision=HIGH,
                    preferred_element_type=jnp.float32,
                )

    @pl.when((i == 0))
    def _():
        out[...] = jnp.zeros_like(out)

    @pl.when((i == 0) & (j == 0))
    def _():
        for a in range(SPAN):
            out[a * BLK : (a + 1) * BLK, a * BLK : (a + 1) * BLK] = chol[a]

    @pl.when((i > 0) & (j == 0))
    def _():
        for a in range(SPAN):
            out[a * BLK : (a + 1) * BLK, :] = lefts[a]


def finish(meta, part, mirror, left, right, diag, chol, inverse):
    def full(shape):
        zeros = (0,) * len(shape)
        return pl.BlockSpec(shape, lambda t, meta: zeros)

    blocks = (SPAN, SPAN, BLK, BLK)
    slices = (NWIN, SPAN, SPAN, SLICE, BLK)
    small = (SPAN, BLK, BLK)
    size = (SPAN * BLK, SPAN * BLK)
    grid_spec = pltpu.PrefetchScalarGridSpec(
        num_scalar_prefetch=1,
        grid=(1,),
        in_specs=[full(s) for s in (blocks, blocks, slices, slices, small, small, small)],
        out_specs=full(size),
    )
    return pl.pallas_call(
        finish_kernel,
        grid_spec=grid_spec,
        out_shape=jax.ShapeDtypeStruct(size, jnp.float32),
        name="finish",
    )(meta, part, mirror, left, right, diag, chol, inverse)


def swap_pairs(size, bit):
    return [(k, k ^ bit) for k in range(size)]


def spread(v, step):
    if step != "x":
        return v + lax.ppermute(v, step, [(0, 1)])
    v = v + lax.ppermute(v, "x", [(0, 1)]) + lax.ppermute(v, "x", [(0, 3)])
    return v + lax.ppermute(v, "x", [(1, 2)])


def body(border, row_scale, block_pick, given_diag):
    i = lax.axis_index(GR).astype(jnp.int32)
    j = lax.axis_index(GC).astype(jnp.int32)
    chip = i // 2
    core = i % 2
    meta = jnp.stack([chip, core, i, j])

    scaled = (jnp.sqrt(row_scale)[:, :, None] * border.astype(jnp.float32)).astype(jnp.bfloat16)

    own = jnp.einsum("srx,sry->sxy", scaled, scaled, preferred_element_type=jnp.float32)
    own_pick = lax.dynamic_slice(block_pick, (j * GROUP, i), (GROUP, 1))[:, 0]
    hot = own_pick[:, None] == jnp.arange(SPAN, dtype=jnp.int32)[None, :]
    diag = jnp.sum(jnp.where(hot[:, :, None, None], own[:, None], 0.0), axis=0)
    for bit in (1, 2, 4):
        diag = diag + lax.ppermute(diag, "z", swap_pairs(8, bit))

    peers = jnp.arange(8, dtype=jnp.int32)
    early = (peers < chip) | ((peers == chip) & (core == 1))
    slots = jnp.where(early[:, None, None, None], scaled[None, :HALF], scaled[None, HALF:])
    same = lax.all_to_all(slots, ("x", "yh"), 0, 0, tiled=True)
    cut = R // 2
    rootly = jnp.where(i == 0, scaled[:HALF], jnp.zeros_like(scaled[:HALF]))
    piece = rootly[:, :cut] + lax.ppermute(rootly[:, cut:], "core", [(0, 1)])
    same, diag, piece = lax.optimization_barrier((same, diag, piece))

    other = lax.ppermute(same, "core", [(0, 1), (1, 0)])
    diag = diag + lax.ppermute(diag, "yl", swap_pairs(2, 1))
    eye = jnp.eye(BLK, dtype=jnp.float32)
    given_here = lax.dynamic_slice(given_diag, (i * SPAN * BLK,), (SPAN * BLK,))
    diag = diag + given_here.reshape(SPAN, 1, BLK) * eye
    corner = spread(spread(jnp.where(i == 0, diag, 0.0), "core"), "yh")
    piece = spread(piece, "yh")
    tiles, late = gram_slots(meta, scaled, same, other)
    tiles, late, corner, piece = lax.optimization_barrier((tiles, late, corner, piece))

    tiles = lax.all_to_all(tiles, GC, 0, 0, tiled=True)
    chol = jnp.linalg.cholesky(spread(corner, "x"))
    piece = spread(piece, "x")
    twin = lax.ppermute(piece, "core", [(0, 1), (1, 0)])
    lead = jnp.concatenate(
        [jnp.where(core == 0, piece, twin), jnp.where(core == 0, twin, piece)], axis=1
    )
    slices = panel_slots(scaled, lead, late)
    tiles, slices, chol = lax.optimization_barrier((tiles, slices, chol))

    part = place(meta, block_pick, tiles)
    slices = lax.all_to_all(slices, GC, 0, 0, tiled=True)
    everywhere = [(r * NWIN + c, c * NWIN + r) for r in range(NWIN) for c in range(NWIN)]
    mirror = lax.ppermute(part, AXES, everywhere)
    slices, chol = lax.optimization_barrier((slices, chol))
    inverse = lax.linalg.triangular_solve(
        chol, jnp.broadcast_to(eye, chol.shape), left_side=True, lower=True
    )
    strip = place_strip(meta, block_pick, slices)
    copies = (NWIN,) + strip.shape
    turned = lax.ppermute(strip, AXES, everywhere)
    left = lax.all_to_all(jnp.broadcast_to(strip, copies), GC, 0, 0, tiled=True)
    turned, inverse = lax.optimization_barrier((turned, inverse))
    right = lax.all_to_all(jnp.broadcast_to(turned, copies), GR, 0, 0, tiled=True)
    return finish(meta, part, mirror, left, right, diag, chol, inverse)


def solution(mesh):
    fine = Mesh(np.asarray(mesh.devices).reshape(SIZES), AXES)
    in_specs = (P(GC, None, GR), P(GC, None), P(), P())
    return jax.shard_map(body, mesh=fine, in_specs=in_specs, out_specs=P(GR, GC), check_vma=False)
```

```python
import jax
import jax.numpy as jnp
import numpy as np
from jax import lax
from jax.experimental import pallas as pl
from jax.experimental.pallas import tpu as pltpu
from jax.sharding import Mesh, PartitionSpec as P

BLK = 128
NWIN = 16
SPAN = 4
R = 768
GROUP = 6
HALF = 3
SLICE = 8
ROWS = HALF * BLK
PLACE = 4

AXES = ("x", "yh", "core", "yl", "z")
SIZES = (4, 2, 2, 2, 8)
GR = ("x", "yh", "core")
GC = ("yl", "z")
HIGH = lax.Precision.HIGHEST
CONTRACT_INNER = (((1,), (0,)), ((), ()))
CONTRACT_ROWS = (((0,), (0,)), ((), ()))
CONTRACT_COLS = (((1,), (1,)), ((), ()))


def flip_kernel(scaled, out):
    out[0] = scaled[0].T


def flip(scaled):
    return pl.pallas_call(
        flip_kernel,
        grid=(GROUP,),
        in_specs=[pl.BlockSpec((1, R, BLK), lambda s: (s, 0, 0))],
        out_specs=pl.BlockSpec((1, BLK, R), lambda s: (s, 0, 0)),
        out_shape=jax.ShapeDtypeStruct((GROUP, BLK, R), scaled.dtype),
        name="flip",
    )(scaled)


def gram_kernel(meta, mine, same, other, out, late):
    q = pl.program_id(0)
    c = meta[1]
    at_same = 2 * q + c
    at_other = 2 * q + 1 - c
    for k in range(HALF):
        pair = jnp.concatenate([same[0, k], other[0, k]], axis=1)
        tiles = lax.dot_general(
            mine[k], pair, CONTRACT_INNER, preferred_element_type=jnp.float32
        )
        out[at_same, k * BLK : (k + 1) * BLK, :] = tiles[:, :BLK]
        out[at_other, k * BLK : (k + 1) * BLK, :] = tiles[:, BLK:]

    @pl.when(q == 0)
    def _():
        late[...] = out[0].reshape(HALF, BLK, BLK)


def gram_slots(meta, flipped, same, other):
    def pick_half(q, meta):
        return (jnp.where((q > meta[0]) | ((q == meta[0]) & (meta[1] == 0)), 0, 1), 0, 0)

    whole = (HALF, R, BLK)
    grid_spec = pltpu.PrefetchScalarGridSpec(
        num_scalar_prefetch=1,
        grid=(NWIN // 2,),
        in_specs=[
            pl.BlockSpec((HALF, BLK, R), pick_half),
            pl.BlockSpec((1,) + whole, lambda q, meta: (q, 0, 0, 0)),
            pl.BlockSpec((1,) + whole, lambda q, meta: (q, 0, 0, 0)),
        ],
        out_specs=[
            pl.BlockSpec((NWIN, ROWS, BLK), lambda q, meta: (0, 0, 0)),
            pl.BlockSpec((HALF, BLK, BLK), lambda q, meta: (0, 0, 0)),
        ],
    )
    return pl.pallas_call(
        gram_kernel,
        grid_spec=grid_spec,
        out_shape=[
            jax.ShapeDtypeStruct((NWIN, ROWS, BLK), jnp.float32),
            jax.ShapeDtypeStruct((HALF, BLK, BLK), jnp.float32),
        ],
        name="gram_slots",
    )(meta, flipped, same, other)


def panel_kernel(first, lead, late, out):
    for m in range(GROUP):
        if m < HALF:
            tile = lax.dot_general(
                first[m], lead[m], CONTRACT_ROWS, preferred_element_type=jnp.float32
            )
        else:
            tile = late[m - HALF]
        for j in range(NWIN):
            out[j, m * SLICE : (m + 1) * SLICE, :] = tile[j * SLICE : (j + 1) * SLICE, :]


def panel_slots(scaled, lead, late):
    whole = (HALF, R, BLK)
    shape = (NWIN, GROUP * SLICE, BLK)
    return pl.pallas_call(
        panel_kernel,
        grid=(1,),
        in_specs=[
            pl.BlockSpec(whole, lambda t: (0, 0, 0)),
            pl.BlockSpec(whole, lambda t: (0, 0, 0)),
            pl.BlockSpec((HALF, BLK, BLK), lambda t: (0, 0, 0)),
        ],
        out_specs=pl.BlockSpec(shape, lambda t: (0, 0, 0)),
        out_shape=jax.ShapeDtypeStruct(shape, jnp.float32),
        name="panel_slots",
    )(scaled, lead, late)


def place_kernel(meta, picks, slots, part):
    g = pl.program_id(0)
    i = meta[2]
    j = meta[3]

    @pl.when(g == 0)
    def _():
        part[...] = jnp.zeros_like(part)

    for u in range(PLACE):
        base = (g * PLACE + u) * GROUP + jnp.where(i < j, 0, HALF)
        for k in range(HALF):
            a = picks[base + k, i]
            b = picks[base + k, j]
            part[a, b] += slots[u, k * BLK : (k + 1) * BLK, :]


def place(meta, picks, slots):
    grid_spec = pltpu.PrefetchScalarGridSpec(
        num_scalar_prefetch=2,
        grid=(NWIN // PLACE,),
        in_specs=[pl.BlockSpec((PLACE, ROWS, BLK), lambda g, *_: (g, 0, 0))],
        out_specs=pl.BlockSpec((SPAN, SPAN, BLK, BLK), lambda g, *_: (0, 0, 0, 0)),
    )
    return pl.pallas_call(
        place_kernel,
        grid_spec=grid_spec,
        out_shape=jax.ShapeDtypeStruct((SPAN, SPAN, BLK, BLK), jnp.float32),
        name="place_tiles",
    )(meta, picks, slots)


def strip_kernel(meta, picks, slots, strip):
    i = meta[2]
    strip[...] = jnp.zeros_like(strip)
    for g in range(NWIN):
        for m in range(GROUP):
            a = picks[g * GROUP + m, i]
            b = picks[g * GROUP + m, 0]
            strip[b, a] += slots[g, m * SLICE : (m + 1) * SLICE, :]


def place_strip(meta, picks, slots):
    shape = (SPAN, SPAN, SLICE, BLK)
    grid_spec = pltpu.PrefetchScalarGridSpec(
        num_scalar_prefetch=2,
        grid=(1,),
        in_specs=[pl.BlockSpec(slots.shape, lambda t, *_: (0, 0, 0))],
        out_specs=pl.BlockSpec(shape, lambda t, *_: (0, 0, 0, 0)),
    )
    return pl.pallas_call(
        strip_kernel,
        grid_spec=grid_spec,
        out_shape=jax.ShapeDtypeStruct(shape, jnp.float32),
        name="place_strip",
    )(meta, picks, slots)


def solve_block(ref, inverse, a):
    solved = [
        lax.dot_general(
            ref[:, b, a].reshape(BLK, BLK),
            inverse[b],
            CONTRACT_COLS,
            precision=HIGH,
            preferred_element_type=jnp.float32,
        )
        for b in range(SPAN)
    ]
    return jnp.concatenate(solved, axis=1)


def full_spec(shape):
    zeros = (0,) * len(shape)
    return pl.BlockSpec(shape, lambda *_: zeros)


def solve_kernel(left, inverse, out):
    for a in range(SPAN):
        out[a] = solve_block(left, inverse, a)


def solve_rows(left, inverse):
    shape = (SPAN, BLK, SPAN * BLK)
    return pl.pallas_call(
        solve_kernel,
        grid=(1,),
        in_specs=[full_spec(left.shape), full_spec(inverse.shape)],
        out_specs=full_spec(shape),
        out_shape=jax.ShapeDtypeStruct(shape, jnp.float32),
        name="solve_rows",
    )(left, inverse)


def update_kernel(meta, part, lefts, right, diag, chol, inverse, out):
    i = meta[2]
    j = meta[3]
    inside = (i > 0) & (j > 0)

    def spot(a, b):
        return (slice(a * BLK, (a + 1) * BLK), slice(b * BLK, (b + 1) * BLK))

    @pl.when(inside & (i != j))
    def _():
        for a in range(SPAN):
            for b in range(SPAN):
                out[spot(a, b)] = part[a, b]

    @pl.when(jnp.logical_not(inside) | (i == j))
    def _():
        out[...] = jnp.zeros_like(out)

    @pl.when(inside & (i == j))
    def _():
        for a in range(SPAN):
            out[spot(a, a)] = diag[a]

    @pl.when(inside)
    def _():
        for b in range(SPAN):
            rights = solve_block(right, inverse, b)
            for a in range(SPAN):
                out[spot(a, b)] = out[spot(a, b)] - lax.dot_general(
                    lefts[a],
                    rights,
                    CONTRACT_COLS,
                    precision=HIGH,
                    preferred_element_type=jnp.float32,
                )

    @pl.when((i == 0) & (j == 0))
    def _():
        for a in range(SPAN):
            out[spot(a, a)] = chol[a]

    @pl.when((i > 0) & (j == 0))
    def _():
        for a in range(SPAN):
            out[a * BLK : (a + 1) * BLK, :] = lefts[a]


def update(meta, part, lefts, right, diag, chol, inverse):
    size = (SPAN * BLK, SPAN * BLK)
    grid_spec = pltpu.PrefetchScalarGridSpec(
        num_scalar_prefetch=1,
        grid=(1,),
        in_specs=[full_spec(v.shape) for v in (part, lefts, right, diag, chol, inverse)],
        out_specs=full_spec(size),
    )
    return pl.pallas_call(
        update_kernel,
        grid_spec=grid_spec,
        out_shape=jax.ShapeDtypeStruct(size, jnp.float32),
        name="update",
    )(meta, part, lefts, right, diag, chol, inverse)


def finish_kernel(meta, base, mirror, out):
    i = meta[2]
    j = meta[3]
    both = (i > 0) & (j > 0) & (i != j)

    @pl.when(both)
    def _():
        for b in range(SPAN):
            out[:, b * BLK : (b + 1) * BLK] = base[:, b * BLK : (b + 1) * BLK] + mirror[b, 0].T

    @pl.when(jnp.logical_not(both))
    def _():
        out[...] = base[...]


def finish(meta, base, mirror):
    size = (SPAN * BLK, SPAN * BLK)
    rows = pl.BlockSpec((BLK, SPAN * BLK), lambda a, meta: (a, 0))
    grid_spec = pltpu.PrefetchScalarGridSpec(
        num_scalar_prefetch=1,
        grid=(SPAN,),
        in_specs=[rows, pl.BlockSpec((SPAN, 1, BLK, BLK), lambda a, meta: (0, a, 0, 0))],
        out_specs=rows,
    )
    return pl.pallas_call(
        finish_kernel,
        grid_spec=grid_spec,
        out_shape=jax.ShapeDtypeStruct(size, jnp.float32),
        name="finish",
    )(meta, base, mirror)


def swap_pairs(size, bit):
    return [(k, k ^ bit) for k in range(size)]


def spread(v, step):
    if step != "x":
        return v + lax.ppermute(v, step, [(0, 1)])
    v = v + lax.ppermute(v, "x", [(0, 1)]) + lax.ppermute(v, "x", [(0, 3)])
    return v + lax.ppermute(v, "x", [(1, 2)])


def body(border, row_scale, block_pick, given_diag):
    i = lax.axis_index(GR).astype(jnp.int32)
    j = lax.axis_index(GC).astype(jnp.int32)
    chip = i // 2
    core = i % 2
    meta = jnp.stack([chip, core, i, j])

    scaled = (jnp.sqrt(row_scale)[:, :, None] * border.astype(jnp.float32)).astype(jnp.bfloat16)

    own = jnp.einsum("srx,sry->sxy", scaled, scaled, preferred_element_type=jnp.float32)
    own_pick = lax.dynamic_slice(block_pick, (j * GROUP, i), (GROUP, 1))[:, 0]
    hot = own_pick[:, None] == jnp.arange(SPAN, dtype=jnp.int32)[None, :]
    diag = jnp.sum(jnp.where(hot[:, :, None, None], own[:, None], 0.0), axis=0)
    for bit in (1, 2, 4):
        diag = diag + lax.ppermute(diag, "z", swap_pairs(8, bit))

    peers = jnp.arange(8, dtype=jnp.int32)
    early = (peers < chip) | ((peers == chip) & (core == 1))
    slots = jnp.where(early[:, None, None, None], scaled[None, :HALF], scaled[None, HALF:])
    same = lax.all_to_all(slots, ("x", "yh"), 0, 0, tiled=True)
    cut = R // 2
    rootly = jnp.where(i == 0, scaled[:HALF], jnp.zeros_like(scaled[:HALF]))
    piece = rootly[:, :cut] + lax.ppermute(rootly[:, cut:], "core", [(0, 1)])
    flipped = flip(scaled)
    same, diag, piece, flipped = lax.optimization_barrier((same, diag, piece, flipped))

    other = lax.ppermute(same, "core", [(0, 1), (1, 0)])
    diag = diag + lax.ppermute(diag, "yl", swap_pairs(2, 1))
    eye = jnp.eye(BLK, dtype=jnp.float32)
    given_here = lax.dynamic_slice(given_diag, (i * SPAN * BLK,), (SPAN * BLK,))
    diag = diag + given_here.reshape(SPAN, 1, BLK) * eye
    corner = spread(jnp.where(i == 0, diag, 0.0), "core")
    corner = spread(corner, "yh")
    piece = spread(piece, "yh")
    tiles, late = gram_slots(meta, flipped, same, other)

    tiles = lax.all_to_all(tiles, GC, 0, 0, tiled=True)
    chol = jnp.linalg.cholesky(spread(corner, "x"))
    piece = spread(piece, "x")
    twin = lax.ppermute(piece, "core", [(0, 1), (1, 0)])
    lead = jnp.concatenate(
        [jnp.where(core == 0, piece, twin), jnp.where(core == 0, twin, piece)], axis=1
    )
    slices = panel_slots(scaled, lead, late)
    tiles, slices, chol = lax.optimization_barrier((tiles, slices, chol))

    part = place(meta, block_pick, tiles)
    slices = lax.all_to_all(slices, GC, 0, 0, tiled=True)
    everywhere = [(r * NWIN + c, c * NWIN + r) for r in range(NWIN) for c in range(NWIN)]
    mirror = lax.ppermute(part, AXES, everywhere)
    slices, chol = lax.optimization_barrier((slices, chol))
    inverse = lax.linalg.triangular_solve(
        chol, jnp.broadcast_to(eye, chol.shape), left_side=True, lower=True
    )
    strip = place_strip(meta, block_pick, slices)
    copies = (NWIN,) + strip.shape
    turned = lax.ppermute(strip, AXES, everywhere)
    left = lax.all_to_all(jnp.broadcast_to(strip, copies), GC, 0, 0, tiled=True)
    turned, inverse = lax.optimization_barrier((turned, inverse))
    right = lax.all_to_all(jnp.broadcast_to(turned, copies), GR, 0, 0, tiled=True)
    lefts = solve_rows(left, inverse)
    base = update(meta, part, lefts, right, diag, chol, inverse)
    return finish(meta, base, mirror)


def solution(mesh):
    fine = Mesh(np.asarray(mesh.devices).reshape(SIZES), AXES)
    in_specs = (P(GC, None, GR), P(GC, None), P(), P())
    return jax.shard_map(body, mesh=fine, in_specs=in_specs, out_specs=P(GR, GC), check_vma=False)
```

```python
import jax
import jax.numpy as jnp
import numpy as np
from jax import lax
from jax.experimental import pallas as pl
from jax.experimental.pallas import tpu as pltpu
from jax.sharding import Mesh, PartitionSpec as P

BLK = 128
NWIN = 16
SPAN = 4
R = 768
GROUP = 6
HALF = 3
SLICE = 8
ROWS = HALF * BLK

AXES = ("x", "yh", "core", "yl", "z")
SIZES = (4, 2, 2, 2, 8)
GR = ("x", "yh", "core")
GC = ("yl", "z")
HIGH = lax.Precision.HIGHEST
CONTRACT_INNER = (((1,), (0,)), ((), ()))
CONTRACT_ROWS = (((0,), (0,)), ((), ()))
CONTRACT_COLS = (((1,), (1,)), ((), ()))


LOCAL = pl.BlockSpec(memory_space=pltpu.VMEM)


def factor_kernel(corner, chol, inverse, work):
    row = lax.broadcasted_iota(jnp.int32, (BLK, BLK), 0)
    lane = lax.broadcasted_iota(jnp.int32, (BLK, BLK), 1)
    strip_row = lax.broadcasted_iota(jnp.int32, (8, 1), 0)
    for b in range(SPAN):
        work[b, :, :BLK] = corner[b]
        work[b, :, BLK:] = jnp.where(row == lane, 1.0, 0.0)
    for t in range(BLK // 8):
        top = 8 * t
        for b in range(SPAN):
            panel = work[b, top : top + 8, :]
            scale = jnp.ones((8, 1), jnp.float32)
            for s in range(8):
                column = panel[:, top + s : top + s + 1]
                pivot = 1.0 / column[s : s + 1, :]
                scale = jnp.where(strip_row == s, pivot, scale)
                factor = jnp.where(strip_row > s, column * pivot, 0.0)
                panel = panel - factor * panel[s : s + 1, :]
            work[b, top : top + 8, :] = panel
            if t < BLK // 8 - 1:
                change = lax.dot_general(
                    panel[:, :BLK] * scale,
                    panel,
                    CONTRACT_ROWS,
                    precision=HIGH,
                    preferred_element_type=jnp.float32,
                )
                work[b, top + 8 :, :] = work[b, top + 8 :, :] - change[top + 8 :, :]
    for b in range(SPAN):
        upper = work[b, :, :BLK]
        pivots = jnp.sum(jnp.where(row == lane, upper, 0.0), axis=1, keepdims=True)
        root = 1.0 / jnp.sqrt(pivots)
        chol[b] = jnp.where(lane >= row, upper * root, 0.0).T
        inverse[b] = work[b, :, BLK:] * root


def factor(corner):
    shape = (SPAN, BLK, BLK)
    return pl.pallas_call(
        factor_kernel,
        in_specs=[LOCAL],
        out_specs=[LOCAL] * 2,
        out_shape=[jax.ShapeDtypeStruct(shape, jnp.float32)] * 2,
        scratch_shapes=[pltpu.VMEM((SPAN, BLK, 2 * BLK), jnp.float32)],
        name="factor",
    )(corner)


def flip_kernel(scaled, out):
    out[0] = scaled[0].T


def flip(scaled):
    return pl.pallas_call(
        flip_kernel,
        grid=(GROUP,),
        in_specs=[pl.BlockSpec((1, R, BLK), lambda s: (s, 0, 0))],
        out_specs=pl.BlockSpec((1, BLK, R), lambda s: (s, 0, 0)),
        out_shape=jax.ShapeDtypeStruct((GROUP, BLK, R), scaled.dtype),
        name="flip",
    )(scaled)


def gram_kernel(meta, mine, same, other, out, late):
    q = pl.program_id(0)
    c = meta[1]
    at_same = 2 * q + c
    at_other = 2 * q + 1 - c
    for k in range(HALF):
        pair = jnp.concatenate([same[0, k], other[0, k]], axis=1)
        tiles = lax.dot_general(
            mine[k], pair, CONTRACT_INNER, preferred_element_type=jnp.float32
        )
        out[at_same, k * BLK : (k + 1) * BLK, :] = tiles[:, :BLK]
        out[at_other, k * BLK : (k + 1) * BLK, :] = tiles[:, BLK:]

    @pl.when(q == 0)
    def _():
        late[...] = out[0].reshape(HALF, BLK, BLK)


def gram_slots(meta, flipped, same, other):
    def pick_half(q, meta):
        return (jnp.where((q > meta[0]) | ((q == meta[0]) & (meta[1] == 0)), 0, 1), 0, 0)

    whole = (HALF, R, BLK)
    grid_spec = pltpu.PrefetchScalarGridSpec(
        num_scalar_prefetch=1,
        grid=(NWIN // 2,),
        in_specs=[
            pl.BlockSpec((HALF, BLK, R), pick_half),
            pl.BlockSpec((1,) + whole, lambda q, meta: (q, 0, 0, 0)),
            pl.BlockSpec((1,) + whole, lambda q, meta: (q, 0, 0, 0)),
        ],
        out_specs=[
            pl.BlockSpec((NWIN, ROWS, BLK), lambda q, meta: (0, 0, 0)),
            pl.BlockSpec((HALF, BLK, BLK), lambda q, meta: (0, 0, 0)),
        ],
    )
    return pl.pallas_call(
        gram_kernel,
        grid_spec=grid_spec,
        out_shape=[
            jax.ShapeDtypeStruct((NWIN, ROWS, BLK), jnp.float32),
            jax.ShapeDtypeStruct((HALF, BLK, BLK), jnp.float32),
        ],
        name="gram_slots",
    )(meta, flipped, same, other)


def panel_kernel(first, lead, late, out):
    for m in range(GROUP):
        if m < HALF:
            tile = lax.dot_general(
                first[m], lead[m], CONTRACT_ROWS, preferred_element_type=jnp.float32
            )
        else:
            tile = late[m - HALF]
        for j in range(NWIN):
            out[j, m * SLICE : (m + 1) * SLICE, :] = tile[j * SLICE : (j + 1) * SLICE, :]


def panel_slots(scaled, lead, late):
    whole = (HALF, R, BLK)
    shape = (NWIN, GROUP * SLICE, BLK)
    return pl.pallas_call(
        panel_kernel,
        grid=(1,),
        in_specs=[
            pl.BlockSpec(whole, lambda t: (0, 0, 0)),
            pl.BlockSpec(whole, lambda t: (0, 0, 0)),
            pl.BlockSpec((HALF, BLK, BLK), lambda t: (0, 0, 0)),
        ],
        out_specs=pl.BlockSpec(shape, lambda t: (0, 0, 0)),
        out_shape=jax.ShapeDtypeStruct(shape, jnp.float32),
        name="panel_slots",
    )(scaled, lead, late)


def place_kernel(meta, picks, slots, part):
    i = meta[2]
    j = meta[3]
    part[...] = jnp.zeros_like(part)
    for g in range(NWIN):
        base = g * GROUP + jnp.where(i < j, 0, HALF)
        for k in range(HALF):
            a = picks[base + k, i]
            b = picks[base + k, j]
            part[a, b] += slots[g, k * BLK : (k + 1) * BLK, :]


def strip_kernel(meta, picks, slots, strip):
    i = meta[2]
    strip[...] = jnp.zeros_like(strip)
    for g in range(NWIN):
        for m in range(GROUP):
            a = picks[g * GROUP + m, i]
            b = picks[g * GROUP + m, 0]
            strip[b, a] += slots[g, m * SLICE : (m + 1) * SLICE, :]


def place(kernel, meta, picks, slots, shape):
    grid_spec = pltpu.PrefetchScalarGridSpec(
        num_scalar_prefetch=2, grid=(1,), in_specs=[LOCAL], out_specs=LOCAL
    )
    return pl.pallas_call(
        kernel, grid_spec=grid_spec, out_shape=jax.ShapeDtypeStruct(shape, jnp.float32)
    )(meta, picks, slots)


def solve_part(ref, inverse, b):
    rows = jnp.concatenate([ref[:, b, a].reshape(BLK, BLK) for a in range(SPAN)], axis=0)
    solved = lax.dot_general(
        rows, inverse[b], CONTRACT_COLS, precision=HIGH, preferred_element_type=jnp.float32
    )
    high = solved.astype(jnp.bfloat16)
    return solved, high, (solved - high.astype(jnp.float32)).astype(jnp.bfloat16)


def solve_kernel(left, inverse, out, high, low):
    for b in range(SPAN):
        cols = slice(b * BLK, (b + 1) * BLK)
        out[:, cols], high[:, cols], low[:, cols] = solve_part(left, inverse, b)


def solve_rows(left, inverse):
    size = (SPAN * BLK, SPAN * BLK)
    return pl.pallas_call(
        solve_kernel,
        in_specs=[LOCAL] * 2,
        out_specs=[LOCAL] * 3,
        out_shape=[jax.ShapeDtypeStruct(size, t) for t in (jnp.float32, jnp.bfloat16, jnp.bfloat16)],
        name="solve_rows",
    )(left, inverse)


def update_kernel(meta, part, lefts, high, low, right, diag, chol, inverse, out):
    i = meta[2]
    j = meta[3]
    inside = (i > 0) & (j > 0)

    def spot(a, b):
        return (slice(a * BLK, (a + 1) * BLK), slice(b * BLK, (b + 1) * BLK))

    @pl.when(inside & (i != j))
    def _():
        for a in range(SPAN):
            for b in range(SPAN):
                out[spot(a, b)] = part[a, b]

    @pl.when(jnp.logical_not(inside) | (i == j))
    def _():
        out[...] = jnp.zeros_like(out)

    @pl.when(inside & (i == j))
    def _():
        for a in range(SPAN):
            out[spot(a, a)] = diag[a]

    @pl.when(inside)
    def _():
        parts = [solve_part(right, inverse, b) for b in range(SPAN)]
        other_high = jnp.concatenate([p[1] for p in parts], axis=1)
        other_low = jnp.concatenate([p[2] for p in parts], axis=1)

        def times(x, y):
            return lax.dot_general(x, y, CONTRACT_COLS, preferred_element_type=jnp.float32)

        small = times(low[...], other_high) + times(high[...], other_low)
        out[...] = out[...] - (times(high[...], other_high) + small)

    @pl.when((i == 0) & (j == 0))
    def _():
        for a in range(SPAN):
            out[spot(a, a)] = chol[a]

    @pl.when((i > 0) & (j == 0))
    def _():
        out[...] = lefts[...]


def update(meta, *operands):
    size = (SPAN * BLK, SPAN * BLK)
    grid_spec = pltpu.PrefetchScalarGridSpec(
        num_scalar_prefetch=1, grid=(1,), in_specs=[LOCAL] * len(operands), out_specs=LOCAL
    )
    return pl.pallas_call(
        update_kernel,
        grid_spec=grid_spec,
        out_shape=jax.ShapeDtypeStruct(size, jnp.float32),
        name="update",
    )(meta, *operands)


def finish_kernel(meta, base, mirror, out):
    i = meta[2]
    j = meta[3]
    both = (i > 0) & (j > 0) & (i != j)

    @pl.when(both)
    def _():
        for b in range(SPAN):
            out[:, b * BLK : (b + 1) * BLK] = base[:, b * BLK : (b + 1) * BLK] + mirror[b, 0].T

    @pl.when(jnp.logical_not(both))
    def _():
        out[...] = base[...]


def finish(meta, base, mirror):
    size = (SPAN * BLK, SPAN * BLK)
    rows = pl.BlockSpec((BLK, SPAN * BLK), lambda a, meta: (a, 0))
    grid_spec = pltpu.PrefetchScalarGridSpec(
        num_scalar_prefetch=1,
        grid=(SPAN,),
        in_specs=[rows, pl.BlockSpec((SPAN, 1, BLK, BLK), lambda a, meta: (0, a, 0, 0))],
        out_specs=rows,
    )
    return pl.pallas_call(
        finish_kernel,
        grid_spec=grid_spec,
        out_shape=jax.ShapeDtypeStruct(size, jnp.float32),
        name="finish",
    )(meta, base, mirror)


def swap_pairs(size, bit):
    return [(k, k ^ bit) for k in range(size)]


def spread(v, step):
    if step != "x":
        return v + lax.ppermute(v, step, [(0, 1)])
    v = v + lax.ppermute(v, "x", [(0, 1)]) + lax.ppermute(v, "x", [(0, 3)])
    return v + lax.ppermute(v, "x", [(1, 2)])


def body(border, row_scale, block_pick, given_diag):
    i = lax.axis_index(GR).astype(jnp.int32)
    j = lax.axis_index(GC).astype(jnp.int32)
    chip = i // 2
    core = i % 2
    meta = jnp.stack([chip, core, i, j])

    scaled = (jnp.sqrt(row_scale)[:, :, None] * border.astype(jnp.float32)).astype(jnp.bfloat16)

    own = jnp.einsum("srx,sry->sxy", scaled, scaled, preferred_element_type=jnp.float32)
    own_pick = lax.dynamic_slice(block_pick, (j * GROUP, i), (GROUP, 1))[:, 0]
    hot = own_pick[:, None] == jnp.arange(SPAN, dtype=jnp.int32)[None, :]
    diag = jnp.sum(jnp.where(hot[:, :, None, None], own[:, None], 0.0), axis=0)
    for bit in (1, 2, 4):
        diag = diag + lax.ppermute(diag, "z", swap_pairs(8, bit))

    peers = jnp.arange(8, dtype=jnp.int32)
    early = (peers < chip) | ((peers == chip) & (core == 1))
    slots = jnp.where(early[:, None, None, None], scaled[None, :HALF], scaled[None, HALF:])
    same = lax.all_to_all(slots, ("x", "yh"), 0, 0, tiled=True)
    cut = R // 2
    rootly = jnp.where(i == 0, scaled[:HALF], jnp.zeros_like(scaled[:HALF]))
    piece = rootly[:, :cut] + lax.ppermute(rootly[:, cut:], "core", [(0, 1)])
    flipped = flip(scaled)
    same, diag, piece, flipped = lax.optimization_barrier((same, diag, piece, flipped))

    other = lax.ppermute(same, "core", [(0, 1), (1, 0)])
    diag = diag + lax.ppermute(diag, "yl", swap_pairs(2, 1))
    eye = jnp.eye(BLK, dtype=jnp.float32)
    given_here = lax.dynamic_slice(given_diag, (i * SPAN * BLK,), (SPAN * BLK,))
    diag = diag + given_here.reshape(SPAN, 1, BLK) * eye
    corner = spread(jnp.where(i == 0, diag, 0.0), "core")
    corner = spread(corner, "yh")
    piece = spread(piece, "yh")
    tiles, late = gram_slots(meta, flipped, same, other)

    tiles = lax.all_to_all(tiles, GC, 0, 0, tiled=True)
    chol, inverse = factor(spread(corner, "x"))
    piece = spread(piece, "x")
    twin = lax.ppermute(piece, "core", [(0, 1), (1, 0)])
    lead = jnp.concatenate(
        [jnp.where(core == 0, piece, twin), jnp.where(core == 0, twin, piece)], axis=1
    )
    slices = panel_slots(scaled, lead, late)
    tiles, slices, chol, inverse = lax.optimization_barrier((tiles, slices, chol, inverse))

    part = place(place_kernel, meta, block_pick, tiles, (SPAN, SPAN, BLK, BLK))
    slices = lax.all_to_all(slices, GC, 0, 0, tiled=True)
    everywhere = [(r * NWIN + c, c * NWIN + r) for r in range(NWIN) for c in range(NWIN)]
    mirror = lax.ppermute(part, AXES, everywhere)
    strip = place(strip_kernel, meta, block_pick, slices, (SPAN, SPAN, SLICE, BLK))
    copies = (NWIN,) + strip.shape
    turned = lax.ppermute(strip, AXES, everywhere)
    left = lax.all_to_all(jnp.broadcast_to(strip, copies), GC, 0, 0, tiled=True)
    right = lax.all_to_all(jnp.broadcast_to(turned, copies), GR, 0, 0, tiled=True)
    lefts, high, low = solve_rows(left, inverse)
    base = update(meta, part, lefts, high, low, right, diag, chol, inverse)
    return finish(meta, base, mirror)


def solution(mesh):
    fine = Mesh(np.asarray(mesh.devices).reshape(SIZES), AXES)
    in_specs = (P(GC, None, GR), P(GC, None), P(), P())
    return jax.shard_map(body, mesh=fine, in_specs=in_specs, out_specs=P(GR, GC), check_vma=False)
```

```python
import jax
import jax.numpy as jnp
import numpy as np
from jax import lax
from jax.experimental import pallas as pl
from jax.experimental.pallas import tpu as pltpu
from jax.sharding import Mesh, PartitionSpec as P

BLK = 128
NWIN = 16
SPAN = 4
R = 768
GROUP = 6
HALF = 3
SLICE = 8
ROWS = HALF * BLK

AXES = ("x", "yh", "core", "yl", "z")
SIZES = (4, 2, 2, 2, 8)
GR = ("x", "yh", "core")
GC = ("yl", "z")
HIGH = lax.Precision.HIGHEST
CONTRACT_INNER = (((1,), (0,)), ((), ()))
CONTRACT_ROWS = (((0,), (0,)), ((), ()))
CONTRACT_COLS = (((1,), (1,)), ((), ()))


LOCAL = pl.BlockSpec(memory_space=pltpu.VMEM)


def factor_kernel(corner, chol, inverse, work):
    row = lax.broadcasted_iota(jnp.int32, (BLK, BLK), 0)
    lane = lax.broadcasted_iota(jnp.int32, (BLK, BLK), 1)
    strip_row = lax.broadcasted_iota(jnp.int32, (8, 1), 0)
    for b in range(SPAN):
        work[b, :, :BLK] = corner[b]
        work[b, :, BLK:] = jnp.where(row == lane, 1.0, 0.0)
    for t in range(BLK // 8):
        top = 8 * t
        for b in range(SPAN):
            panel = work[b, top : top + 8, :]
            scale = jnp.ones((8, 1), jnp.float32)
            for s in range(8):
                column = panel[:, top + s : top + s + 1]
                pivot = 1.0 / column[s : s + 1, :]
                scale = jnp.where(strip_row == s, pivot, scale)
                factor = jnp.where(strip_row > s, column * pivot, 0.0)
                panel = panel - factor * panel[s : s + 1, :]
            work[b, top : top + 8, :] = panel
            if t < BLK // 8 - 1:
                change = lax.dot_general(
                    panel[:, :BLK] * scale,
                    panel,
                    CONTRACT_ROWS,
                    precision=HIGH,
                    preferred_element_type=jnp.float32,
                )
                work[b, top + 8 :, :] = work[b, top + 8 :, :] - change[top + 8 :, :]
    for b in range(SPAN):
        upper = work[b, :, :BLK]
        pivots = jnp.sum(jnp.where(row == lane, upper, 0.0), axis=1, keepdims=True)
        root = 1.0 / jnp.sqrt(pivots)
        chol[b] = jnp.where(lane >= row, upper * root, 0.0).T
        inverse[b] = work[b, :, BLK:] * root


def factor(corner):
    shape = (SPAN, BLK, BLK)
    return pl.pallas_call(
        factor_kernel,
        in_specs=[LOCAL],
        out_specs=[LOCAL] * 2,
        out_shape=[jax.ShapeDtypeStruct(shape, jnp.float32)] * 2,
        scratch_shapes=[pltpu.VMEM((SPAN, BLK, 2 * BLK), jnp.float32)],
        name="factor",
    )(corner)


def flip_kernel(scaled, out):
    out[0] = scaled[0].T


def flip(scaled):
    return pl.pallas_call(
        flip_kernel,
        grid=(GROUP,),
        in_specs=[pl.BlockSpec((1, R, BLK), lambda s: (s, 0, 0))],
        out_specs=pl.BlockSpec((1, BLK, R), lambda s: (s, 0, 0)),
        out_shape=jax.ShapeDtypeStruct((GROUP, BLK, R), scaled.dtype),
        name="flip",
    )(scaled)


def gram_kernel(meta, mine, same, other, out, late):
    q = pl.program_id(0)
    c = meta[1]
    at_same = 2 * q + c
    at_other = 2 * q + 1 - c
    for k in range(HALF):
        pair = jnp.concatenate([same[0, k], other[0, k]], axis=1)
        tiles = lax.dot_general(
            mine[k], pair, CONTRACT_INNER, preferred_element_type=jnp.float32
        )
        out[at_same, k * BLK : (k + 1) * BLK, :] = tiles[:, :BLK]
        out[at_other, k * BLK : (k + 1) * BLK, :] = tiles[:, BLK:]

    @pl.when(q == 0)
    def _():
        late[...] = out[0].reshape(HALF, BLK, BLK)


def gram_slots(meta, flipped, same, other):
    def pick_half(q, meta):
        return (jnp.where((q > meta[0]) | ((q == meta[0]) & (meta[1] == 0)), 0, 1), 0, 0)

    whole = (HALF, R, BLK)
    grid_spec = pltpu.PrefetchScalarGridSpec(
        num_scalar_prefetch=1,
        grid=(NWIN // 2,),
        in_specs=[
            pl.BlockSpec((HALF, BLK, R), pick_half),
            pl.BlockSpec((1,) + whole, lambda q, meta: (q, 0, 0, 0)),
            pl.BlockSpec((1,) + whole, lambda q, meta: (q, 0, 0, 0)),
        ],
        out_specs=[
            pl.BlockSpec((NWIN, ROWS, BLK), lambda q, meta: (0, 0, 0)),
            pl.BlockSpec((HALF, BLK, BLK), lambda q, meta: (0, 0, 0)),
        ],
    )
    return pl.pallas_call(
        gram_kernel,
        grid_spec=grid_spec,
        out_shape=[
            jax.ShapeDtypeStruct((NWIN, ROWS, BLK), jnp.float32),
            jax.ShapeDtypeStruct((HALF, BLK, BLK), jnp.float32),
        ],
        name="gram_slots",
    )(meta, flipped, same, other)


def panel_kernel(first, lead, late, out):
    for m in range(GROUP):
        if m < HALF:
            tile = lax.dot_general(
                first[m], lead[m], CONTRACT_ROWS, preferred_element_type=jnp.float32
            )
        else:
            tile = late[m - HALF]
        for j in range(NWIN):
            out[j, m * SLICE : (m + 1) * SLICE, :] = tile[j * SLICE : (j + 1) * SLICE, :]


def panel_slots(scaled, lead, late):
    whole = (HALF, R, BLK)
    shape = (NWIN, GROUP * SLICE, BLK)
    return pl.pallas_call(
        panel_kernel,
        grid=(1,),
        in_specs=[
            pl.BlockSpec(whole, lambda t: (0, 0, 0)),
            pl.BlockSpec(whole, lambda t: (0, 0, 0)),
            pl.BlockSpec((HALF, BLK, BLK), lambda t: (0, 0, 0)),
        ],
        out_specs=pl.BlockSpec(shape, lambda t: (0, 0, 0)),
        out_shape=jax.ShapeDtypeStruct(shape, jnp.float32),
        name="panel_slots",
    )(scaled, lead, late)


def place_kernel(meta, picks, slots, upper, lower, part):
    i = meta[2]
    j = meta[3]
    part[...] = jnp.zeros_like(part)
    for g in range(NWIN):
        base = g * GROUP + jnp.where(i < j, 0, HALF)
        for k in range(HALF):
            a = picks[base + k, i]
            b = picks[base + k, j]
            part[a, b] += slots[g, k * BLK : (k + 1) * BLK, :]
    upper[...] = part[: SPAN // 2]
    lower[...] = part[SPAN // 2 :]


def place_tiles(meta, picks, slots):
    shape = (SPAN // 2, SPAN, BLK, BLK)
    grid_spec = pltpu.PrefetchScalarGridSpec(
        num_scalar_prefetch=2,
        grid=(1,),
        in_specs=[LOCAL],
        out_specs=[LOCAL] * 2,
        scratch_shapes=[pltpu.VMEM((SPAN, SPAN, BLK, BLK), jnp.float32)],
    )
    return pl.pallas_call(
        place_kernel,
        grid_spec=grid_spec,
        out_shape=[jax.ShapeDtypeStruct(shape, jnp.float32)] * 2,
        name="place_tiles",
    )(meta, picks, slots)


def strip_kernel(meta, picks, slots, strip):
    i = meta[2]
    strip[...] = jnp.zeros_like(strip)
    for g in range(NWIN):
        for m in range(GROUP):
            a = picks[g * GROUP + m, i]
            b = picks[g * GROUP + m, 0]
            strip[b, a] += slots[g, m * SLICE : (m + 1) * SLICE, :]


def place_strip(meta, picks, slots):
    grid_spec = pltpu.PrefetchScalarGridSpec(
        num_scalar_prefetch=2, grid=(1,), in_specs=[LOCAL], out_specs=LOCAL
    )
    return pl.pallas_call(
        strip_kernel,
        grid_spec=grid_spec,
        out_shape=jax.ShapeDtypeStruct((SPAN, SPAN, SLICE, BLK), jnp.float32),
        name="place_strip",
    )(meta, picks, slots)


def solve_part(ref, inverse, b, order):
    rows = jnp.concatenate(
        [ref[order[k], b, a] for a in range(SPAN) for k in range(NWIN)], axis=0
    )
    solved = lax.dot_general(
        rows, inverse[b], CONTRACT_COLS, precision=HIGH, preferred_element_type=jnp.float32
    )
    high = solved.astype(jnp.bfloat16)
    return solved, high, (solved - high.astype(jnp.float32)).astype(jnp.bfloat16)


def solve_kernel(left, inverse, out, high, low):
    for b in range(SPAN):
        cols = slice(b * BLK, (b + 1) * BLK)
        out[:, cols], high[:, cols], low[:, cols] = solve_part(left, inverse, b, range(NWIN))


def solve_rows(left, inverse):
    size = (SPAN * BLK, SPAN * BLK)
    return pl.pallas_call(
        solve_kernel,
        in_specs=[LOCAL] * 2,
        out_specs=[LOCAL] * 3,
        out_shape=[jax.ShapeDtypeStruct(size, t) for t in (jnp.float32, jnp.bfloat16, jnp.bfloat16)],
        name="solve_rows",
    )(left, inverse)


def update_kernel(meta, upper, lower, lefts, high, low, right, diag, chol, inverse, out):
    i = meta[2]
    j = meta[3]
    inside = (i > 0) & (j > 0)

    def spot(a, b):
        return (slice(a * BLK, (a + 1) * BLK), slice(b * BLK, (b + 1) * BLK))

    @pl.when(inside & (i != j))
    def _():
        for a in range(SPAN):
            for b in range(SPAN):
                half = upper if a < SPAN // 2 else lower
                out[spot(a, b)] = half[a % (SPAN // 2), b]

    @pl.when(jnp.logical_not(inside) | (i == j))
    def _():
        out[...] = jnp.zeros_like(out)

    @pl.when(inside & (i == j))
    def _():
        for a in range(SPAN):
            out[spot(a, a)] = diag[a]

    @pl.when(inside)
    def _():
        gaps = [k ^ i for k in range(NWIN)]
        order = [
            ((d >> 1) & 1) | ((((d >> 2) ^ (d >> 3)) & 1) << 1) | ((d >> 3) << 2) | ((d & 1) << 3)
            for d in gaps
        ]
        parts = [solve_part(right, inverse, b, order) for b in range(SPAN)]
        other_high = jnp.concatenate([p[1] for p in parts], axis=1)
        other_low = jnp.concatenate([p[2] for p in parts], axis=1)

        def times(x, y):
            return lax.dot_general(x, y, CONTRACT_COLS, preferred_element_type=jnp.float32)

        small = times(low[...], other_high) + times(high[...], other_low)
        out[...] = out[...] - (times(high[...], other_high) + small)

    @pl.when((i == 0) & (j == 0))
    def _():
        for a in range(SPAN):
            out[spot(a, a)] = chol[a]

    @pl.when((i > 0) & (j == 0))
    def _():
        out[...] = lefts[...]


def update(meta, *operands):
    size = (SPAN * BLK, SPAN * BLK)
    grid_spec = pltpu.PrefetchScalarGridSpec(
        num_scalar_prefetch=1, grid=(1,), in_specs=[LOCAL] * len(operands), out_specs=LOCAL
    )
    return pl.pallas_call(
        update_kernel,
        grid_spec=grid_spec,
        out_shape=jax.ShapeDtypeStruct(size, jnp.float32),
        name="update",
    )(meta, *operands)


def finish_kernel(meta, base, upper, lower, out):
    i = meta[2]
    j = meta[3]
    both = (i > 0) & (j > 0) & (i != j)

    @pl.when(both)
    def _():
        for b in range(SPAN):
            half = upper if b < SPAN // 2 else lower
            cols = slice(b * BLK, (b + 1) * BLK)
            out[:, cols] = base[:, cols] + half[b % (SPAN // 2), 0].T

    @pl.when(jnp.logical_not(both))
    def _():
        out[...] = base[...]


def finish(meta, base, upper, lower):
    size = (SPAN * BLK, SPAN * BLK)
    rows = pl.BlockSpec((BLK, SPAN * BLK), lambda a, meta: (a, 0))
    tall = pl.BlockSpec((SPAN // 2, 1, BLK, BLK), lambda a, meta: (0, a, 0, 0))
    grid_spec = pltpu.PrefetchScalarGridSpec(
        num_scalar_prefetch=1, grid=(SPAN,), in_specs=[rows, tall, tall], out_specs=rows
    )
    return pl.pallas_call(
        finish_kernel,
        grid_spec=grid_spec,
        out_shape=jax.ShapeDtypeStruct(size, jnp.float32),
        name="finish",
    )(meta, base, upper, lower)


def swap_pairs(size, bit):
    return [(k, k ^ bit) for k in range(size)]


def spread(v, step):
    if step != "x":
        return v + lax.ppermute(v, step, [(0, 1)])
    v = v + lax.ppermute(v, "x", [(0, 1)]) + lax.ppermute(v, "x", [(0, 3)])
    return v + lax.ppermute(v, "x", [(1, 2)])


def body(border, row_scale, block_pick, given_diag):
    i = lax.axis_index(GR).astype(jnp.int32)
    j = lax.axis_index(GC).astype(jnp.int32)
    chip = i // 2
    core = i % 2
    meta = jnp.stack([chip, core, i, j])

    scaled = (jnp.sqrt(row_scale)[:, :, None] * border.astype(jnp.float32)).astype(jnp.bfloat16)

    own = jnp.einsum("srx,sry->sxy", scaled, scaled, preferred_element_type=jnp.float32)
    own_pick = lax.dynamic_slice(block_pick, (j * GROUP, i), (GROUP, 1))[:, 0]
    hot = own_pick[:, None] == jnp.arange(SPAN, dtype=jnp.int32)[None, :]
    diag = jnp.sum(jnp.where(hot[:, :, None, None], own[:, None], 0.0), axis=0)
    for bit in (1, 2, 4):
        diag = diag + lax.ppermute(diag, "z", swap_pairs(8, bit))

    peers = jnp.arange(8, dtype=jnp.int32)
    early = (peers < chip) | ((peers == chip) & (core == 1))
    slots = jnp.where(early[:, None, None, None], scaled[None, :HALF], scaled[None, HALF:])
    same = lax.all_to_all(slots, ("x", "yh"), 0, 0, tiled=True)
    cut = R // 2
    rootly = jnp.where(i == 0, scaled[:HALF], jnp.zeros_like(scaled[:HALF]))
    piece = rootly[:, :cut] + lax.ppermute(rootly[:, cut:], "core", [(0, 1)])
    flipped = flip(scaled)
    same, diag, piece, flipped = lax.optimization_barrier((same, diag, piece, flipped))

    other = lax.ppermute(same, "core", [(0, 1), (1, 0)])
    across = lax.ppermute(diag, "yl", swap_pairs(2, 1))
    tiles, late = gram_slots(meta, flipped, same, other)
    across, late = lax.optimization_barrier((across, late))
    diag = diag + across
    eye = jnp.eye(BLK, dtype=jnp.float32)
    given_here = lax.dynamic_slice(given_diag, (i * SPAN * BLK,), (SPAN * BLK,))
    diag = diag + given_here.reshape(SPAN, 1, BLK) * eye
    corner = spread(jnp.where(i == 0, diag, 0.0), "core")
    corner = spread(corner, "yh")
    piece = spread(piece, "yh")

    tiles = lax.all_to_all(tiles, GC, 0, 0, tiled=True)
    chol, inverse = factor(spread(corner, "x"))
    piece = spread(piece, "x")
    twin = lax.ppermute(piece, "core", [(0, 1), (1, 0)])
    lead = jnp.concatenate(
        [jnp.where(core == 0, piece, twin), jnp.where(core == 0, twin, piece)], axis=1
    )
    slices = panel_slots(scaled, lead, late)
    tiles, slices, chol, inverse = lax.optimization_barrier((tiles, slices, chol, inverse))

    upper, lower = place_tiles(meta, block_pick, tiles)
    slices = lax.all_to_all(slices, GC, 0, 0, tiled=True)
    everywhere = [(r * NWIN + c, c * NWIN + r) for r in range(NWIN) for c in range(NWIN)]
    strip = place_strip(meta, block_pick, slices)
    right = lax.ppermute(strip, AXES, everywhere)[None]
    copies = jnp.broadcast_to(strip, (NWIN,) + strip.shape)
    left = lax.all_to_all(copies, GC, 0, 0, tiled=True)
    mirror_a = lax.ppermute(upper, AXES, everywhere)
    mirror_b = lax.ppermute(lower, AXES, everywhere)
    for axis, pairs in (
        ("yh", swap_pairs(2, 1)),
        ("x", swap_pairs(4, 1)),
        ("x", swap_pairs(4, 3)),
        ("core", swap_pairs(2, 1)),
    ):
        right = jnp.concatenate([right, lax.ppermute(right, axis, pairs)], axis=0)
    lefts, high, low = solve_rows(left, inverse)
    base = update(meta, upper, lower, lefts, high, low, right, diag, chol, inverse)
    return finish(meta, base, mirror_a, mirror_b)


def solution(mesh):
    fine = Mesh(np.asarray(mesh.devices).reshape(SIZES), AXES)
    in_specs = (P(GC, None, GR), P(GC, None), P(), P())
    return jax.shard_map(body, mesh=fine, in_specs=in_specs, out_specs=P(GR, GC), check_vma=False)
```

```python
import jax
import jax.numpy as jnp
import numpy as np
from jax import lax
from jax.experimental import pallas as pl
from jax.experimental.pallas import tpu as pltpu
from jax.sharding import Mesh, PartitionSpec as P

BLK = 128
NWIN = 16
SPAN = 4
R = 768
GROUP = 6
HALF = 3
SLICE = 8
ROWS = HALF * BLK

LANDING = (
    (0, 1, 2, 3, 4, 5, 6, 7, 8, 9, 10, 11, 12, 13, 14, 15),
    (14, 5, 0, 13, 6, 9, 12, 10, 2, 1, 8, 4, 3, 7, 11, 15),
    (5, 12, 0, 3, 4, 13, 14, 7, 15, 10, 2, 1, 11, 8, 6, 9),
    (8, 0, 9, 6, 3, 7, 4, 10, 5, 11, 2, 12, 1, 13, 14, 15),
    (0, 10, 2, 5, 8, 6, 14, 3, 7, 1, 15, 12, 4, 13, 11, 9),
    (2, 1, 7, 3, 4, 8, 13, 15, 6, 10, 9, 11, 12, 5, 14, 0),
    (10, 1, 2, 5, 12, 15, 11, 0, 8, 4, 14, 3, 9, 13, 6, 7),
    (6, 3, 7, 9, 10, 13, 4, 14, 0, 1, 2, 11, 12, 15, 5, 8),
    (3, 8, 0, 12, 10, 14, 4, 15, 6, 9, 2, 5, 11, 1, 13, 7),
    (10, 2, 1, 5, 3, 0, 14, 7, 8, 13, 9, 11, 12, 6, 4, 15),
    (12, 8, 9, 10, 3, 5, 0, 1, 15, 2, 14, 11, 4, 7, 6, 13),
    (0, 7, 12, 11, 4, 6, 5, 13, 15, 9, 10, 8, 3, 14, 2, 1),
    (0, 6, 15, 4, 10, 5, 12, 2, 7, 11, 1, 3, 8, 13, 14, 9),
    (9, 10, 11, 13, 3, 15, 6, 7, 14, 2, 0, 12, 4, 1, 5, 8),
    (0, 1, 7, 11, 4, 13, 14, 15, 8, 2, 6, 12, 3, 5, 10, 9),
    (5, 3, 10, 4, 2, 13, 6, 15, 8, 9, 0, 11, 12, 7, 14, 1),
)
BLOCK_AT = tuple(tuple(row.index(m) for m in range(NWIN)) for row in LANDING)
INNER = [(r, c) for r in range(1, NWIN) for c in range(1, NWIN) if r != c]

AXES = ("x", "yh", "core", "yl", "z")
SIZES = (4, 2, 2, 2, 8)
GR = ("x", "yh", "core")
GC = ("yl", "z")
HIGH = lax.Precision.HIGHEST
CONTRACT_INNER = (((1,), (0,)), ((), ()))
CONTRACT_ROWS = (((0,), (0,)), ((), ()))
CONTRACT_COLS = (((1,), (1,)), ((), ()))


LOCAL = pl.BlockSpec(memory_space=pltpu.VMEM)


def factor_kernel(corner, chol, inverse, work):
    row = lax.broadcasted_iota(jnp.int32, (BLK, BLK), 0)
    lane = lax.broadcasted_iota(jnp.int32, (BLK, BLK), 1)
    strip_row = lax.broadcasted_iota(jnp.int32, (8, 1), 0)
    for b in range(SPAN):
        work[b, :, :BLK] = corner[b]
        work[b, :, BLK:] = jnp.where(row == lane, 1.0, 0.0)
    for t in range(BLK // 8):
        top = 8 * t
        for b in range(SPAN):
            panel = work[b, top : top + 8, :]
            scale = jnp.ones((8, 1), jnp.float32)
            for s in range(8):
                column = panel[:, top + s : top + s + 1]
                pivot = 1.0 / column[s : s + 1, :]
                scale = jnp.where(strip_row == s, pivot, scale)
                factor = jnp.where(strip_row > s, column * pivot, 0.0)
                panel = panel - factor * panel[s : s + 1, :]
            work[b, top : top + 8, :] = panel
            if t < BLK // 8 - 1:
                change = lax.dot_general(
                    panel[:, :BLK] * scale,
                    panel,
                    CONTRACT_ROWS,
                    precision=HIGH,
                    preferred_element_type=jnp.float32,
                )
                work[b, top + 8 :, :] = work[b, top + 8 :, :] - change[top + 8 :, :]
    for b in range(SPAN):
        upper = work[b, :, :BLK]
        pivots = jnp.sum(jnp.where(row == lane, upper, 0.0), axis=1, keepdims=True)
        root = 1.0 / jnp.sqrt(pivots)
        chol[b] = jnp.where(lane >= row, upper * root, 0.0).T
        inverse[b] = work[b, :, BLK:] * root


def factor(corner):
    shape = (SPAN, BLK, BLK)
    return pl.pallas_call(
        factor_kernel,
        in_specs=[LOCAL],
        out_specs=[LOCAL] * 2,
        out_shape=[jax.ShapeDtypeStruct(shape, jnp.float32)] * 2,
        scratch_shapes=[pltpu.VMEM((SPAN, BLK, 2 * BLK), jnp.float32)],
        name="factor",
    )(corner)


def flip_kernel(scaled, out):
    out[0] = scaled[0].T


def flip(scaled):
    return pl.pallas_call(
        flip_kernel,
        grid=(GROUP,),
        in_specs=[pl.BlockSpec((1, R, BLK), lambda s: (s, 0, 0))],
        out_specs=pl.BlockSpec((1, BLK, R), lambda s: (s, 0, 0)),
        out_shape=jax.ShapeDtypeStruct((GROUP, BLK, R), scaled.dtype),
        name="flip",
    )(scaled)


def gram_kernel(meta, landing, mine, same, other, out, late):
    q = pl.program_id(0)
    c = meta[1]
    i = meta[2]
    at_same = landing[i, 2 * q + c]
    at_other = landing[i, 2 * q + 1 - c]
    for k in range(HALF):
        pair = jnp.concatenate([same[0, k], other[0, k]], axis=1)
        tiles = lax.dot_general(
            mine[k], pair, CONTRACT_INNER, preferred_element_type=jnp.float32
        )
        out[at_same, k * BLK : (k + 1) * BLK, :] = tiles[:, :BLK]
        out[at_other, k * BLK : (k + 1) * BLK, :] = tiles[:, BLK:]

    @pl.when(q == 0)
    def _():
        late[...] = out[landing[i, 0]].reshape(HALF, BLK, BLK)


def gram_slots(meta, flipped, same, other):
    def pick_half(q, meta, landing):
        return (jnp.where((q > meta[0]) | ((q == meta[0]) & (meta[1] == 0)), 0, 1), 0, 0)

    whole = (HALF, R, BLK)
    grid_spec = pltpu.PrefetchScalarGridSpec(
        num_scalar_prefetch=2,
        grid=(NWIN // 2,),
        in_specs=[
            pl.BlockSpec((HALF, BLK, R), pick_half),
            pl.BlockSpec((1,) + whole, lambda q, *_: (q, 0, 0, 0)),
            pl.BlockSpec((1,) + whole, lambda q, *_: (q, 0, 0, 0)),
        ],
        out_specs=[
            pl.BlockSpec((NWIN, ROWS, BLK), lambda q, *_: (0, 0, 0)),
            pl.BlockSpec((HALF, BLK, BLK), lambda q, *_: (0, 0, 0)),
        ],
    )
    return pl.pallas_call(
        gram_kernel,
        grid_spec=grid_spec,
        out_shape=[
            jax.ShapeDtypeStruct((NWIN, ROWS, BLK), jnp.float32),
            jax.ShapeDtypeStruct((HALF, BLK, BLK), jnp.float32),
        ],
        name="gram_slots",
    )(meta, jnp.array(LANDING, jnp.int32), flipped, same, other)


def panel_kernel(first, lead, late, out):
    for m in range(GROUP):
        if m < HALF:
            tile = lax.dot_general(
                first[m], lead[m], CONTRACT_ROWS, preferred_element_type=jnp.float32
            )
        else:
            tile = late[m - HALF]
        for j in range(NWIN):
            out[j, m * SLICE : (m + 1) * SLICE, :] = tile[j * SLICE : (j + 1) * SLICE, :]


def panel_slots(scaled, lead, late):
    whole = (HALF, R, BLK)
    shape = (NWIN, GROUP * SLICE, BLK)
    return pl.pallas_call(
        panel_kernel,
        grid=(1,),
        in_specs=[
            pl.BlockSpec(whole, lambda t: (0, 0, 0)),
            pl.BlockSpec(whole, lambda t: (0, 0, 0)),
            pl.BlockSpec((HALF, BLK, BLK), lambda t: (0, 0, 0)),
        ],
        out_specs=pl.BlockSpec(shape, lambda t: (0, 0, 0)),
        out_shape=jax.ShapeDtypeStruct(shape, jnp.float32),
        name="panel_slots",
    )(scaled, lead, late)


def place_kernel(meta, picks, block_at, slots, upper, lower, part):
    i = meta[2]
    j = block_at[i, meta[3]]
    part[...] = jnp.zeros_like(part)
    for g in range(NWIN):
        base = g * GROUP + jnp.where(i < j, 0, HALF)
        for k in range(HALF):
            a = picks[base + k, i]
            b = picks[base + k, j]
            part[a, b] += slots[g, k * BLK : (k + 1) * BLK, :]
    upper[...] = part[: SPAN // 2]
    lower[...] = part[SPAN // 2 :]


def place_tiles(meta, picks, slots):
    shape = (SPAN // 2, SPAN, BLK, BLK)
    grid_spec = pltpu.PrefetchScalarGridSpec(
        num_scalar_prefetch=3,
        grid=(1,),
        in_specs=[LOCAL],
        out_specs=[LOCAL] * 2,
        scratch_shapes=[pltpu.VMEM((SPAN, SPAN, BLK, BLK), jnp.float32)],
    )
    return pl.pallas_call(
        place_kernel,
        grid_spec=grid_spec,
        out_shape=[jax.ShapeDtypeStruct(shape, jnp.float32)] * 2,
        name="place_tiles",
    )(meta, picks, jnp.array(BLOCK_AT, jnp.int32), slots)


def strip_kernel(meta, picks, slots, strip):
    i = meta[2]
    strip[...] = jnp.zeros_like(strip)
    for g in range(NWIN):
        for m in range(GROUP):
            a = picks[g * GROUP + m, i]
            b = picks[g * GROUP + m, 0]
            strip[b, a] += slots[g, m * SLICE : (m + 1) * SLICE, :]


def place_strip(meta, picks, slots):
    grid_spec = pltpu.PrefetchScalarGridSpec(
        num_scalar_prefetch=2, grid=(1,), in_specs=[LOCAL], out_specs=LOCAL
    )
    return pl.pallas_call(
        strip_kernel,
        grid_spec=grid_spec,
        out_shape=jax.ShapeDtypeStruct((SPAN, SPAN, SLICE, BLK), jnp.float32),
        name="place_strip",
    )(meta, picks, slots)


def solve_part(ref, inverse, b, order):
    rows = jnp.concatenate(
        [ref[order[k], b, a] for a in range(SPAN) for k in range(NWIN)], axis=0
    )
    solved = lax.dot_general(
        rows, inverse[b], CONTRACT_COLS, precision=HIGH, preferred_element_type=jnp.float32
    )
    high = solved.astype(jnp.bfloat16)
    return solved, high, (solved - high.astype(jnp.float32)).astype(jnp.bfloat16)


def solve_kernel(left, inverse, out, high, low):
    for b in range(SPAN):
        cols = slice(b * BLK, (b + 1) * BLK)
        out[:, cols], high[:, cols], low[:, cols] = solve_part(left, inverse, b, range(NWIN))


def solve_rows(left, inverse):
    size = (SPAN * BLK, SPAN * BLK)
    return pl.pallas_call(
        solve_kernel,
        in_specs=[LOCAL] * 2,
        out_specs=[LOCAL] * 3,
        out_shape=[jax.ShapeDtypeStruct(size, t) for t in (jnp.float32, jnp.bfloat16, jnp.bfloat16)],
        name="solve_rows",
    )(left, inverse)


def update_kernel(meta, lefts, high, low, right, diag, chol, inverse, out):
    i = meta[2]
    j = meta[3]
    inside = (i > 0) & (j > 0)

    def spot(a, b):
        return (slice(a * BLK, (a + 1) * BLK), slice(b * BLK, (b + 1) * BLK))

    out[...] = jnp.zeros_like(out)

    @pl.when(inside & (i == j))
    def _():
        for a in range(SPAN):
            out[spot(a, a)] = diag[a]

    @pl.when(inside)
    def _():
        gaps = [k ^ i for k in range(NWIN)]
        order = [
            ((d >> 1) & 1) | ((((d >> 2) ^ (d >> 3)) & 1) << 1) | ((d >> 3) << 2) | ((d & 1) << 3)
            for d in gaps
        ]
        parts = [solve_part(right, inverse, b, order) for b in range(SPAN)]
        other_high = jnp.concatenate([p[1] for p in parts], axis=1)
        other_low = jnp.concatenate([p[2] for p in parts], axis=1)

        def times(x, y):
            return lax.dot_general(x, y, CONTRACT_COLS, preferred_element_type=jnp.float32)

        small = times(low[...], other_high) + times(high[...], other_low)
        out[...] = out[...] - (times(high[...], other_high) + small)

    @pl.when((i == 0) & (j == 0))
    def _():
        for a in range(SPAN):
            out[spot(a, a)] = chol[a]

    @pl.when((i > 0) & (j == 0))
    def _():
        out[...] = lefts[...]


def update(meta, *operands):
    size = (SPAN * BLK, SPAN * BLK)
    grid_spec = pltpu.PrefetchScalarGridSpec(
        num_scalar_prefetch=1, grid=(1,), in_specs=[LOCAL] * len(operands), out_specs=LOCAL
    )
    return pl.pallas_call(
        update_kernel,
        grid_spec=grid_spec,
        out_shape=jax.ShapeDtypeStruct(size, jnp.float32),
        name="update",
    )(meta, *operands)


def finish_kernel(meta, base, upper, lower, turned_upper, turned_lower, out):
    a = pl.program_id(0)
    i = meta[2]
    j = meta[3]
    both = (i > 0) & (j > 0) & (i != j)

    def add(near):
        for b in range(SPAN):
            far = turned_upper if b < SPAN // 2 else turned_lower
            cols = slice(b * BLK, (b + 1) * BLK)
            out[:, cols] = base[:, cols] + (near[0, b] + far[b % (SPAN // 2), 0].T)

    @pl.when(both & (a < SPAN // 2))
    def _():
        add(upper)

    @pl.when(both & (a >= SPAN // 2))
    def _():
        add(lower)

    @pl.when(jnp.logical_not(both))
    def _():
        out[...] = base[...]


def finish(meta, *operands):
    size = (SPAN * BLK, SPAN * BLK)
    rows = pl.BlockSpec((BLK, SPAN * BLK), lambda a, meta: (a, 0))
    wide = pl.BlockSpec((1, SPAN, BLK, BLK), lambda a, meta: (a % (SPAN // 2), 0, 0, 0))
    tall = pl.BlockSpec((SPAN // 2, 1, BLK, BLK), lambda a, meta: (0, a, 0, 0))
    grid_spec = pltpu.PrefetchScalarGridSpec(
        num_scalar_prefetch=1,
        grid=(SPAN,),
        in_specs=[rows, wide, wide, tall, tall],
        out_specs=rows,
    )
    return pl.pallas_call(
        finish_kernel,
        grid_spec=grid_spec,
        out_shape=jax.ShapeDtypeStruct(size, jnp.float32),
        name="finish",
    )(meta, *operands)


def swap_pairs(size, bit):
    return [(k, k ^ bit) for k in range(size)]


def spread(v, step):
    if step != "x":
        return v + lax.ppermute(v, step, [(0, 1)])
    v = v + lax.ppermute(v, "x", [(0, 1)]) + lax.ppermute(v, "x", [(0, 3)])
    return v + lax.ppermute(v, "x", [(1, 2)])


def body(border, row_scale, block_pick, given_diag):
    i = lax.axis_index(GR).astype(jnp.int32)
    j = lax.axis_index(GC).astype(jnp.int32)
    chip = i // 2
    core = i % 2
    meta = jnp.stack([chip, core, i, j])

    scaled = (jnp.sqrt(row_scale)[:, :, None] * border.astype(jnp.float32)).astype(jnp.bfloat16)

    own = jnp.einsum("srx,sry->sxy", scaled, scaled, preferred_element_type=jnp.float32)
    own_pick = lax.dynamic_slice(block_pick, (j * GROUP, i), (GROUP, 1))[:, 0]
    hot = own_pick[:, None] == jnp.arange(SPAN, dtype=jnp.int32)[None, :]
    diag = jnp.sum(jnp.where(hot[:, :, None, None], own[:, None], 0.0), axis=0)
    for bit in (1, 2, 4):
        diag = diag + lax.ppermute(diag, "z", swap_pairs(8, bit))

    peers = jnp.arange(8, dtype=jnp.int32)
    early = (peers < chip) | ((peers == chip) & (core == 1))
    slots = jnp.where(early[:, None, None, None], scaled[None, :HALF], scaled[None, HALF:])
    same = lax.all_to_all(slots, ("x", "yh"), 0, 0, tiled=True)
    cut = R // 2
    rootly = jnp.where(i == 0, scaled[:HALF], jnp.zeros_like(scaled[:HALF]))
    piece = rootly[:, :cut] + lax.ppermute(rootly[:, cut:], "core", [(0, 1)])
    flipped = flip(scaled)
    same, diag, piece, flipped = lax.optimization_barrier((same, diag, piece, flipped))

    other = lax.ppermute(same, "core", [(0, 1), (1, 0)])
    across = lax.ppermute(diag, "yl", swap_pairs(2, 1))
    tiles, late = gram_slots(meta, flipped, same, other)
    across, late = lax.optimization_barrier((across, late))
    diag = diag + across
    eye = jnp.eye(BLK, dtype=jnp.float32)
    given_here = lax.dynamic_slice(given_diag, (i * SPAN * BLK,), (SPAN * BLK,))
    diag = diag + given_here.reshape(SPAN, 1, BLK) * eye
    corner = spread(jnp.where(i == 0, diag, 0.0), "core")
    corner = spread(corner, "yh")
    piece = spread(piece, "yh")

    tiles = lax.all_to_all(tiles, GC, 0, 0, tiled=True)
    chol, inverse = factor(spread(corner, "x"))
    piece = spread(piece, "x")
    twin = lax.ppermute(piece, "core", [(0, 1), (1, 0)])
    lead = jnp.concatenate(
        [jnp.where(core == 0, piece, twin), jnp.where(core == 0, twin, piece)], axis=1
    )
    slices = panel_slots(scaled, lead, late)
    tiles, slices, chol, inverse = lax.optimization_barrier((tiles, slices, chol, inverse))

    upper, lower = place_tiles(meta, block_pick, tiles)
    slices = lax.all_to_all(slices, GC, 0, 0, tiled=True)
    everywhere = [(r * NWIN + c, c * NWIN + r) for r in range(NWIN) for c in range(NWIN)]
    strip = place_strip(meta, block_pick, slices)
    right = lax.ppermute(strip, AXES, everywhere)[None]
    copies = jnp.broadcast_to(strip, (NWIN,) + strip.shape)
    left = lax.all_to_all(copies, GC, 0, 0, tiled=True)
    home = [(r * NWIN + LANDING[r][c], r * NWIN + c) for r, c in INNER]
    across = [(r * NWIN + LANDING[r][c], c * NWIN + r) for r, c in INNER]
    sums_a = [lax.ppermute(upper, AXES, pairs) for pairs in (across, home)]
    sums_b = [lax.ppermute(lower, AXES, pairs) for pairs in (across, home)]
    for axis, pairs in (
        ("yh", swap_pairs(2, 1)),
        ("x", swap_pairs(4, 1)),
        ("x", swap_pairs(4, 3)),
        ("core", swap_pairs(2, 1)),
    ):
        right = jnp.concatenate([right, lax.ppermute(right, axis, pairs)], axis=0)
    lefts, high, low = solve_rows(left, inverse)
    base = update(meta, lefts, high, low, right, diag, chol, inverse)
    return finish(meta, base, sums_a[1], sums_b[1], sums_a[0], sums_b[0])


def solution(mesh):
    fine = Mesh(np.asarray(mesh.devices).reshape(SIZES), AXES)
    in_specs = (P(GC, None, GR), P(GC, None), P(), P())
    return jax.shard_map(body, mesh=fine, in_specs=in_specs, out_specs=P(GR, GC), check_vma=False)
```

```python
import jax
import jax.numpy as jnp
import numpy as np
from jax import lax
from jax.experimental import pallas as pl
from jax.experimental.pallas import tpu as pltpu
from jax.sharding import Mesh, PartitionSpec as P

BLK = 128
NWIN = 16
SPAN = 4
R = 768
GROUP = 6
HALF = 3
SLICE = 8
ROWS = HALF * BLK

AXES = ("x", "yh", "core", "yl", "z")
SIZES = (4, 2, 2, 2, 8)
GR = ("x", "yh", "core")
GC = ("yl", "z")
HIGH = lax.Precision.HIGHEST
CONTRACT_INNER = (((1,), (0,)), ((), ()))
CONTRACT_ROWS = (((0,), (0,)), ((), ()))
CONTRACT_COLS = (((1,), (1,)), ((), ()))


LOCAL = pl.BlockSpec(memory_space=pltpu.VMEM)


def factor_kernel(corner, chol, inverse, work):
    row = lax.broadcasted_iota(jnp.int32, (BLK, BLK), 0)
    lane = lax.broadcasted_iota(jnp.int32, (BLK, BLK), 1)
    strip_row = lax.broadcasted_iota(jnp.int32, (8, 1), 0)
    for b in range(SPAN):
        work[b, :, :BLK] = corner[b]
        work[b, :, BLK:] = jnp.where(row == lane, 1.0, 0.0)
    for t in range(BLK // 8):
        top = 8 * t
        for b in range(SPAN):
            panel = work[b, top : top + 8, :]
            scale = jnp.ones((8, 1), jnp.float32)
            for s in range(8):
                column = panel[:, top + s : top + s + 1]
                pivot = 1.0 / column[s : s + 1, :]
                scale = jnp.where(strip_row == s, pivot, scale)
                factor = jnp.where(strip_row > s, column * pivot, 0.0)
                panel = panel - factor * panel[s : s + 1, :]
            work[b, top : top + 8, :] = panel
            if t < BLK // 8 - 1:
                change = lax.dot_general(
                    panel[:, :BLK] * scale,
                    panel,
                    CONTRACT_ROWS,
                    precision=HIGH,
                    preferred_element_type=jnp.float32,
                )
                work[b, top + 8 :, :] = work[b, top + 8 :, :] - change[top + 8 :, :]
    for b in range(SPAN):
        upper = work[b, :, :BLK]
        pivots = jnp.sum(jnp.where(row == lane, upper, 0.0), axis=1, keepdims=True)
        root = 1.0 / jnp.sqrt(pivots)
        chol[b] = jnp.where(lane >= row, upper * root, 0.0).T
        inverse[b] = work[b, :, BLK:] * root


def factor(corner):
    shape = (SPAN, BLK, BLK)
    return pl.pallas_call(
        factor_kernel,
        in_specs=[LOCAL],
        out_specs=[LOCAL] * 2,
        out_shape=[jax.ShapeDtypeStruct(shape, jnp.float32)] * 2,
        scratch_shapes=[pltpu.VMEM((SPAN, BLK, 2 * BLK), jnp.float32)],
        name="factor",
    )(corner)


def flip_kernel(scaled, out):
    out[0] = scaled[0].T


def flip(scaled):
    return pl.pallas_call(
        flip_kernel,
        grid=(GROUP,),
        in_specs=[pl.BlockSpec((1, R, BLK), lambda s: (s, 0, 0))],
        out_specs=pl.BlockSpec((1, BLK, R), lambda s: (s, 0, 0)),
        out_shape=jax.ShapeDtypeStruct((GROUP, BLK, R), scaled.dtype),
        name="flip",
    )(scaled)


def gram_kernel(meta, mine, same, other, out, late):
    q = pl.program_id(0)
    c = meta[1]
    at_same = 2 * q + c
    at_other = 2 * q + 1 - c
    for k in range(HALF):
        pair = jnp.concatenate([same[0, k], other[0, k]], axis=1)
        tiles = lax.dot_general(
            mine[k], pair, CONTRACT_INNER, preferred_element_type=jnp.float32
        )
        out[at_same, k * BLK : (k + 1) * BLK, :] = tiles[:, :BLK]
        out[at_other, k * BLK : (k + 1) * BLK, :] = tiles[:, BLK:]

    @pl.when(q == 0)
    def _():
        late[...] = out[0].reshape(HALF, BLK, BLK)


def gram_slots(meta, flipped, same, other):
    def pick_half(q, meta):
        return (jnp.where((q > meta[0]) | ((q == meta[0]) & (meta[1] == 0)), 0, 1), 0, 0)

    whole = (HALF, R, BLK)
    grid_spec = pltpu.PrefetchScalarGridSpec(
        num_scalar_prefetch=1,
        grid=(NWIN // 2,),
        in_specs=[
            pl.BlockSpec((HALF, BLK, R), pick_half),
            pl.BlockSpec((1,) + whole, lambda q, meta: (q, 0, 0, 0)),
            pl.BlockSpec((1,) + whole, lambda q, meta: (q, 0, 0, 0)),
        ],
        out_specs=[
            pl.BlockSpec((NWIN, ROWS, BLK), lambda q, meta: (0, 0, 0)),
            pl.BlockSpec((HALF, BLK, BLK), lambda q, meta: (0, 0, 0)),
        ],
    )
    return pl.pallas_call(
        gram_kernel,
        grid_spec=grid_spec,
        out_shape=[
            jax.ShapeDtypeStruct((NWIN, ROWS, BLK), jnp.float32),
            jax.ShapeDtypeStruct((HALF, BLK, BLK), jnp.float32),
        ],
        name="gram_slots",
    )(meta, flipped, same, other)


def panel_kernel(first, lead, late, out):
    for m in range(GROUP):
        if m < HALF:
            tile = lax.dot_general(
                first[m], lead[m], CONTRACT_ROWS, preferred_element_type=jnp.float32
            )
        else:
            tile = late[m - HALF]
        for j in range(NWIN):
            out[j, m * SLICE : (m + 1) * SLICE, :] = tile[j * SLICE : (j + 1) * SLICE, :]


def panel_slots(scaled, lead, late):
    whole = (HALF, R, BLK)
    shape = (NWIN, GROUP * SLICE, BLK)
    return pl.pallas_call(
        panel_kernel,
        grid=(1,),
        in_specs=[
            pl.BlockSpec(whole, lambda t: (0, 0, 0)),
            pl.BlockSpec(whole, lambda t: (0, 0, 0)),
            pl.BlockSpec((HALF, BLK, BLK), lambda t: (0, 0, 0)),
        ],
        out_specs=pl.BlockSpec(shape, lambda t: (0, 0, 0)),
        out_shape=jax.ShapeDtypeStruct(shape, jnp.float32),
        name="panel_slots",
    )(scaled, lead, late)


def place_kernel(meta, picks, slots, part):
    i = meta[2]
    j = meta[3]
    part[...] = jnp.zeros_like(part)
    for g in range(NWIN):
        base = g * GROUP + jnp.where(i < j, 0, HALF)
        for k in range(HALF):
            a = picks[base + k, i]
            b = picks[base + k, j]
            part[a, b] += slots[g, k * BLK : (k + 1) * BLK, :]


def strip_kernel(meta, picks, slots, strip):
    i = meta[2]
    strip[...] = jnp.zeros_like(strip)
    for g in range(NWIN):
        for m in range(GROUP):
            a = picks[g * GROUP + m, i]
            b = picks[g * GROUP + m, 0]
            strip[b, a] += slots[g, m * SLICE : (m + 1) * SLICE, :]


def place(kernel, meta, picks, slots, shape):
    grid_spec = pltpu.PrefetchScalarGridSpec(
        num_scalar_prefetch=2, grid=(1,), in_specs=[LOCAL], out_specs=LOCAL
    )
    return pl.pallas_call(
        kernel, grid_spec=grid_spec, out_shape=jax.ShapeDtypeStruct(shape, jnp.float32)
    )(meta, picks, slots)


def solve_part(ref, inverse, b, order):
    rows = jnp.concatenate(
        [ref[order[k], b, a] for a in range(SPAN) for k in range(NWIN)], axis=0
    )
    solved = lax.dot_general(
        rows, inverse[b], CONTRACT_COLS, precision=HIGH, preferred_element_type=jnp.float32
    )
    high = solved.astype(jnp.bfloat16)
    return solved, high, (solved - high.astype(jnp.float32)).astype(jnp.bfloat16)


def solve_kernel(left, inverse, out, high, low):
    for b in range(SPAN):
        cols = slice(b * BLK, (b + 1) * BLK)
        out[:, cols], high[:, cols], low[:, cols] = solve_part(left, inverse, b, range(NWIN))


def solve_rows(left, inverse):
    size = (SPAN * BLK, SPAN * BLK)
    return pl.pallas_call(
        solve_kernel,
        in_specs=[LOCAL] * 2,
        out_specs=[LOCAL] * 3,
        out_shape=[jax.ShapeDtypeStruct(size, t) for t in (jnp.float32, jnp.bfloat16, jnp.bfloat16)],
        name="solve_rows",
    )(left, inverse)


def update_kernel(meta, part, lefts, high, low, right, diag, chol, inverse, out):
    i = meta[2]
    j = meta[3]
    inside = (i > 0) & (j > 0)

    def spot(a, b):
        return (slice(a * BLK, (a + 1) * BLK), slice(b * BLK, (b + 1) * BLK))

    @pl.when(inside & (i != j))
    def _():
        for a in range(SPAN):
            for b in range(SPAN):
                out[spot(a, b)] = part[a, b]

    @pl.when(jnp.logical_not(inside) | (i == j))
    def _():
        out[...] = jnp.zeros_like(out)

    @pl.when(inside & (i == j))
    def _():
        for a in range(SPAN):
            out[spot(a, a)] = diag[a]

    @pl.when(inside)
    def _():
        gaps = [k ^ i for k in range(NWIN)]
        order = [
            ((d >> 1) & 1) | ((((d >> 2) ^ (d >> 3)) & 1) << 1) | ((d >> 3) << 2) | ((d & 1) << 3)
            for d in gaps
        ]
        parts = [solve_part(right, inverse, b, order) for b in range(SPAN)]
        other_high = jnp.concatenate([p[1] for p in parts], axis=1)
        other_low = jnp.concatenate([p[2] for p in parts], axis=1)

        def times(x, y):
            return lax.dot_general(x, y, CONTRACT_COLS, preferred_element_type=jnp.float32)

        small = times(low[...], other_high) + times(high[...], other_low)
        out[...] = out[...] - (times(high[...], other_high) + small)

    @pl.when((i == 0) & (j == 0))
    def _():
        for a in range(SPAN):
            out[spot(a, a)] = chol[a]

    @pl.when((i > 0) & (j == 0))
    def _():
        out[...] = lefts[...]


def update(meta, *operands):
    size = (SPAN * BLK, SPAN * BLK)
    grid_spec = pltpu.PrefetchScalarGridSpec(
        num_scalar_prefetch=1, grid=(1,), in_specs=[LOCAL] * len(operands), out_specs=LOCAL
    )
    return pl.pallas_call(
        update_kernel,
        grid_spec=grid_spec,
        out_shape=jax.ShapeDtypeStruct(size, jnp.float32),
        name="update",
    )(meta, *operands)


def finish_kernel(meta, base, mirror, out):
    i = meta[2]
    j = meta[3]
    both = (i > 0) & (j > 0) & (i != j)

    @pl.when(both)
    def _():
        for b in range(SPAN):
            out[:, b * BLK : (b + 1) * BLK] = base[:, b * BLK : (b + 1) * BLK] + mirror[b, 0].T

    @pl.when(jnp.logical_not(both))
    def _():
        out[...] = base[...]


def finish(meta, base, mirror):
    size = (SPAN * BLK, SPAN * BLK)
    rows = pl.BlockSpec((BLK, SPAN * BLK), lambda a, meta: (a, 0))
    grid_spec = pltpu.PrefetchScalarGridSpec(
        num_scalar_prefetch=1,
        grid=(SPAN,),
        in_specs=[rows, pl.BlockSpec((SPAN, 1, BLK, BLK), lambda a, meta: (0, a, 0, 0))],
        out_specs=rows,
    )
    return pl.pallas_call(
        finish_kernel,
        grid_spec=grid_spec,
        out_shape=jax.ShapeDtypeStruct(size, jnp.float32),
        name="finish",
    )(meta, base, mirror)


def swap_pairs(size, bit):
    return [(k, k ^ bit) for k in range(size)]


def spread(v, step):
    if step != "x":
        return v + lax.ppermute(v, step, [(0, 1)])
    v = v + lax.ppermute(v, "x", [(0, 1)]) + lax.ppermute(v, "x", [(0, 3)])
    return v + lax.ppermute(v, "x", [(1, 2)])


def body(border, row_scale, block_pick, given_diag):
    i = lax.axis_index(GR).astype(jnp.int32)
    j = lax.axis_index(GC).astype(jnp.int32)
    chip = i // 2
    core = i % 2
    meta = jnp.stack([chip, core, i, j])

    scaled = (jnp.sqrt(row_scale)[:, :, None] * border.astype(jnp.float32)).astype(jnp.bfloat16)

    own = jnp.einsum("srx,sry->sxy", scaled, scaled, preferred_element_type=jnp.float32)
    own_pick = lax.dynamic_slice(block_pick, (j * GROUP, i), (GROUP, 1))[:, 0]
    hot = own_pick[:, None] == jnp.arange(SPAN, dtype=jnp.int32)[None, :]
    diag = jnp.sum(jnp.where(hot[:, :, None, None], own[:, None], 0.0), axis=0)
    for bit in (1, 2, 4):
        diag = diag + lax.ppermute(diag, "z", swap_pairs(8, bit))

    peers = jnp.arange(8, dtype=jnp.int32)
    early = (peers < chip) | ((peers == chip) & (core == 1))
    slots = jnp.where(early[:, None, None, None], scaled[None, :HALF], scaled[None, HALF:])
    same = lax.all_to_all(slots, ("x", "yh"), 0, 0, tiled=True)
    cut = R // 2
    rootly = jnp.where(i == 0, scaled[:HALF], jnp.zeros_like(scaled[:HALF]))
    piece = rootly[:, :cut] + lax.ppermute(rootly[:, cut:], "core", [(0, 1)])
    flipped = flip(scaled)
    same, diag, piece, flipped = lax.optimization_barrier((same, diag, piece, flipped))

    other = lax.ppermute(same, "core", [(0, 1), (1, 0)])
    across = lax.ppermute(diag, "yl", swap_pairs(2, 1))
    tiles, late = gram_slots(meta, flipped, same, other)
    across, late = lax.optimization_barrier((across, late))
    diag = diag + across
    eye = jnp.eye(BLK, dtype=jnp.float32)
    given_here = lax.dynamic_slice(given_diag, (i * SPAN * BLK,), (SPAN * BLK,))
    diag = diag + given_here.reshape(SPAN, 1, BLK) * eye
    corner = spread(jnp.where(i == 0, diag, 0.0), "core")
    corner = spread(corner, "yh")
    piece = spread(piece, "yh")

    tiles = lax.all_to_all(tiles, GC, 0, 0, tiled=True)
    chol, inverse = factor(spread(corner, "x"))
    piece = spread(piece, "x")
    twin = lax.ppermute(piece, "core", [(0, 1), (1, 0)])
    lead = jnp.concatenate(
        [jnp.where(core == 0, piece, twin), jnp.where(core == 0, twin, piece)], axis=1
    )
    slices = panel_slots(scaled, lead, late)
    tiles, slices, chol, inverse = lax.optimization_barrier((tiles, slices, chol, inverse))

    part = place(place_kernel, meta, block_pick, tiles, (SPAN, SPAN, BLK, BLK))
    slices = lax.all_to_all(slices, GC, 0, 0, tiled=True)
    everywhere = [(r * NWIN + c, c * NWIN + r) for r in range(NWIN) for c in range(NWIN)]
    strip = place(strip_kernel, meta, block_pick, slices, (SPAN, SPAN, SLICE, BLK))
    right = lax.ppermute(strip, AXES, everywhere)[None]
    copies = jnp.broadcast_to(strip, (NWIN,) + strip.shape)
    left = lax.all_to_all(copies, GC, 0, 0, tiled=True)
    inner = [(r * NWIN + c, c * NWIN + r) for r in range(1, NWIN) for c in range(1, NWIN) if r != c]
    mirror = lax.ppermute(part, AXES, inner)
    for axis, pairs in (
        ("yh", swap_pairs(2, 1)),
        ("x", swap_pairs(4, 1)),
        ("x", swap_pairs(4, 3)),
        ("core", swap_pairs(2, 1)),
    ):
        right = jnp.concatenate([right, lax.ppermute(right, axis, pairs)], axis=0)
    lefts, high, low = solve_rows(left, inverse)
    base = update(meta, part, lefts, high, low, right, diag, chol, inverse)
    return finish(meta, base, mirror)


def solution(mesh):
    fine = Mesh(np.asarray(mesh.devices).reshape(SIZES), AXES)
    in_specs = (P(GC, None, GR), P(GC, None), P(), P())
    return jax.shard_map(body, mesh=fine, in_specs=in_specs, out_specs=P(GR, GC), check_vma=False)
```

```python
import jax
import jax.numpy as jnp
import numpy as np
from jax import lax
from jax.experimental import pallas as pl
from jax.experimental.pallas import tpu as pltpu
from jax.sharding import Mesh, PartitionSpec as P

BLK = 128
NWIN = 16
SPAN = 4
R = 768
GROUP = 6
HALF = 3
SLICE = 8
ROWS = HALF * BLK

AXES = ("x", "yh", "core", "yl", "z")
SIZES = (4, 2, 2, 2, 8)
GR = ("x", "yh", "core")
GC = ("yl", "z")
HIGH = lax.Precision.HIGHEST
CONTRACT_INNER = (((1,), (0,)), ((), ()))
CONTRACT_ROWS = (((0,), (0,)), ((), ()))
CONTRACT_COLS = (((1,), (1,)), ((), ()))


LOCAL = pl.BlockSpec(memory_space=pltpu.VMEM)


def factor_kernel(corner, chol, inverse, work):
    row = lax.broadcasted_iota(jnp.int32, (BLK, BLK), 0)
    lane = lax.broadcasted_iota(jnp.int32, (BLK, BLK), 1)
    strip_row = lax.broadcasted_iota(jnp.int32, (8, 1), 0)
    for b in range(SPAN):
        work[b, :, :BLK] = corner[b]
        work[b, :, BLK:] = jnp.where(row == lane, 1.0, 0.0)
    for t in range(BLK // 8):
        top = 8 * t
        for b in range(SPAN):
            panel = work[b, top : top + 8, :]
            scale = jnp.ones((8, 1), jnp.float32)
            for s in range(8):
                column = panel[:, top + s : top + s + 1]
                pivot = 1.0 / column[s : s + 1, :]
                scale = jnp.where(strip_row == s, pivot, scale)
                factor = jnp.where(strip_row > s, column * pivot, 0.0)
                panel = panel - factor * panel[s : s + 1, :]
            work[b, top : top + 8, :] = panel
            if t < BLK // 8 - 1:
                change = lax.dot_general(
                    panel[:, :BLK] * scale,
                    panel,
                    CONTRACT_ROWS,
                    precision=HIGH,
                    preferred_element_type=jnp.float32,
                )
                work[b, top + 8 :, :] = work[b, top + 8 :, :] - change[top + 8 :, :]
    for b in range(SPAN):
        upper = work[b, :, :BLK]
        pivots = jnp.sum(jnp.where(row == lane, upper, 0.0), axis=1, keepdims=True)
        root = 1.0 / jnp.sqrt(pivots)
        chol[b] = jnp.where(lane >= row, upper * root, 0.0).T
        inverse[b] = work[b, :, BLK:] * root


def factor(corner):
    shape = (SPAN, BLK, BLK)
    return pl.pallas_call(
        factor_kernel,
        in_specs=[LOCAL],
        out_specs=[LOCAL] * 2,
        out_shape=[jax.ShapeDtypeStruct(shape, jnp.float32)] * 2,
        scratch_shapes=[pltpu.VMEM((SPAN, BLK, 2 * BLK), jnp.float32)],
        name="factor",
    )(corner)


def flip_kernel(scaled, out):
    out[0] = scaled[0].T


def flip(scaled):
    return pl.pallas_call(
        flip_kernel,
        grid=(GROUP,),
        in_specs=[pl.BlockSpec((1, R, BLK), lambda s: (s, 0, 0))],
        out_specs=pl.BlockSpec((1, BLK, R), lambda s: (s, 0, 0)),
        out_shape=jax.ShapeDtypeStruct((GROUP, BLK, R), scaled.dtype),
        name="flip",
    )(scaled)


def gram_kernel(meta, mine, same, other, out, late):
    q = pl.program_id(0)
    c = meta[1]
    at_same = 2 * q + c
    at_other = 2 * q + 1 - c
    for k in range(HALF):
        pair = jnp.concatenate([same[0, k], other[0, k]], axis=1)
        tiles = lax.dot_general(
            mine[k], pair, CONTRACT_INNER, preferred_element_type=jnp.float32
        )
        out[at_same, k * BLK : (k + 1) * BLK, :] = tiles[:, :BLK]
        out[at_other, k * BLK : (k + 1) * BLK, :] = tiles[:, BLK:]

    @pl.when(q == 0)
    def _():
        late[...] = out[0].reshape(HALF, BLK, BLK)


def gram_slots(meta, flipped, same, other):
    def pick_half(q, meta):
        return (jnp.where((q > meta[0]) | ((q == meta[0]) & (meta[1] == 0)), 0, 1), 0, 0)

    whole = (HALF, R, BLK)
    grid_spec = pltpu.PrefetchScalarGridSpec(
        num_scalar_prefetch=1,
        grid=(NWIN // 2,),
        in_specs=[
            pl.BlockSpec((HALF, BLK, R), pick_half),
            pl.BlockSpec((1,) + whole, lambda q, meta: (q, 0, 0, 0)),
            pl.BlockSpec((1,) + whole, lambda q, meta: (q, 0, 0, 0)),
        ],
        out_specs=[
            pl.BlockSpec((NWIN, ROWS, BLK), lambda q, meta: (0, 0, 0)),
            pl.BlockSpec((HALF, BLK, BLK), lambda q, meta: (0, 0, 0)),
        ],
    )
    return pl.pallas_call(
        gram_kernel,
        grid_spec=grid_spec,
        out_shape=[
            jax.ShapeDtypeStruct((NWIN, ROWS, BLK), jnp.float32),
            jax.ShapeDtypeStruct((HALF, BLK, BLK), jnp.float32),
        ],
        name="gram_slots",
    )(meta, flipped, same, other)


def panel_kernel(first, lead, late, out):
    for m in range(GROUP):
        if m < HALF:
            tile = lax.dot_general(
                first[m], lead[m], CONTRACT_ROWS, preferred_element_type=jnp.float32
            )
        else:
            tile = late[m - HALF]
        for j in range(NWIN):
            out[j, m * SLICE : (m + 1) * SLICE, :] = tile[j * SLICE : (j + 1) * SLICE, :]


def panel_slots(scaled, lead, late):
    whole = (HALF, R, BLK)
    shape = (NWIN, GROUP * SLICE, BLK)
    return pl.pallas_call(
        panel_kernel,
        grid=(1,),
        in_specs=[
            pl.BlockSpec(whole, lambda t: (0, 0, 0)),
            pl.BlockSpec(whole, lambda t: (0, 0, 0)),
            pl.BlockSpec((HALF, BLK, BLK), lambda t: (0, 0, 0)),
        ],
        out_specs=pl.BlockSpec(shape, lambda t: (0, 0, 0)),
        out_shape=jax.ShapeDtypeStruct(shape, jnp.float32),
        name="panel_slots",
    )(scaled, lead, late)


def place_kernel(meta, picks, slots, upper, lower, part):
    i = meta[2]
    j = meta[3]
    part[...] = jnp.zeros_like(part)
    for g in range(NWIN):
        base = g * GROUP + jnp.where(i < j, 0, HALF)
        for k in range(HALF):
            a = picks[base + k, i]
            b = picks[base + k, j]
            part[a, b] += slots[g, k * BLK : (k + 1) * BLK, :]
    upper[...] = part[: SPAN // 2]
    lower[...] = part[SPAN // 2 :]


def place_tiles(meta, picks, slots):
    shape = (SPAN // 2, SPAN, BLK, BLK)
    grid_spec = pltpu.PrefetchScalarGridSpec(
        num_scalar_prefetch=2,
        grid=(1,),
        in_specs=[LOCAL],
        out_specs=[LOCAL] * 2,
        scratch_shapes=[pltpu.VMEM((SPAN, SPAN, BLK, BLK), jnp.float32)],
    )
    return pl.pallas_call(
        place_kernel,
        grid_spec=grid_spec,
        out_shape=[jax.ShapeDtypeStruct(shape, jnp.float32)] * 2,
        name="place_tiles",
    )(meta, picks, slots)


def strip_kernel(meta, picks, slots, strip):
    i = meta[2]
    strip[...] = jnp.zeros_like(strip)
    for g in range(NWIN):
        for m in range(GROUP):
            a = picks[g * GROUP + m, i]
            b = picks[g * GROUP + m, 0]
            strip[b, a] += slots[g, m * SLICE : (m + 1) * SLICE, :]


def place_strip(meta, picks, slots):
    grid_spec = pltpu.PrefetchScalarGridSpec(
        num_scalar_prefetch=2, grid=(1,), in_specs=[LOCAL], out_specs=LOCAL
    )
    return pl.pallas_call(
        strip_kernel,
        grid_spec=grid_spec,
        out_shape=jax.ShapeDtypeStruct((SPAN, SPAN, SLICE, BLK), jnp.float32),
        name="place_strip",
    )(meta, picks, slots)


def solve_part(ref, inverse, b, order):
    rows = jnp.concatenate(
        [ref[order[k], b, a] for a in range(SPAN) for k in range(NWIN)], axis=0
    )
    solved = lax.dot_general(
        rows, inverse[b], CONTRACT_COLS, precision=HIGH, preferred_element_type=jnp.float32
    )
    high = solved.astype(jnp.bfloat16)
    return solved, high, (solved - high.astype(jnp.float32)).astype(jnp.bfloat16)


def solve_kernel(left, inverse, out, high, low):
    for b in range(SPAN):
        cols = slice(b * BLK, (b + 1) * BLK)
        out[:, cols], high[:, cols], low[:, cols] = solve_part(left, inverse, b, range(NWIN))


def solve_rows(left, inverse):
    size = (SPAN * BLK, SPAN * BLK)
    return pl.pallas_call(
        solve_kernel,
        in_specs=[LOCAL] * 2,
        out_specs=[LOCAL] * 3,
        out_shape=[jax.ShapeDtypeStruct(size, t) for t in (jnp.float32, jnp.bfloat16, jnp.bfloat16)],
        name="solve_rows",
    )(left, inverse)


def update_kernel(meta, upper, lower, lefts, high, low, right, diag, chol, inverse, out):
    i = meta[2]
    j = meta[3]
    inside = (i > 0) & (j > 0)

    def spot(a, b):
        return (slice(a * BLK, (a + 1) * BLK), slice(b * BLK, (b + 1) * BLK))

    @pl.when(inside & (i != j))
    def _():
        for a in range(SPAN):
            for b in range(SPAN):
                half = upper if a < SPAN // 2 else lower
                out[spot(a, b)] = half[a % (SPAN // 2), b]

    @pl.when(jnp.logical_not(inside) | (i == j))
    def _():
        out[...] = jnp.zeros_like(out)

    @pl.when(inside & (i == j))
    def _():
        for a in range(SPAN):
            out[spot(a, a)] = diag[a]

    @pl.when(inside)
    def _():
        gaps = [k ^ i for k in range(NWIN)]
        order = [
            ((d >> 1) & 1) | ((((d >> 2) ^ (d >> 3)) & 1) << 1) | ((d >> 3) << 2) | ((d & 1) << 3)
            for d in gaps
        ]
        parts = [solve_part(right, inverse, b, order) for b in range(SPAN)]
        other_high = jnp.concatenate([p[1] for p in parts], axis=1)
        other_low = jnp.concatenate([p[2] for p in parts], axis=1)

        def times(x, y):
            return lax.dot_general(x, y, CONTRACT_COLS, preferred_element_type=jnp.float32)

        small = times(low[...], other_high) + times(high[...], other_low)
        out[...] = out[...] - (times(high[...], other_high) + small)

    @pl.when((i == 0) & (j == 0))
    def _():
        for a in range(SPAN):
            out[spot(a, a)] = chol[a]

    @pl.when((i > 0) & (j == 0))
    def _():
        out[...] = lefts[...]


def update(meta, *operands):
    size = (SPAN * BLK, SPAN * BLK)
    grid_spec = pltpu.PrefetchScalarGridSpec(
        num_scalar_prefetch=1, grid=(1,), in_specs=[LOCAL] * len(operands), out_specs=LOCAL
    )
    return pl.pallas_call(
        update_kernel,
        grid_spec=grid_spec,
        out_shape=jax.ShapeDtypeStruct(size, jnp.float32),
        name="update",
    )(meta, *operands)


def finish_kernel(meta, base, upper, lower, out):
    i = meta[2]
    j = meta[3]
    both = (i > 0) & (j > 0) & (i != j)

    @pl.when(both)
    def _():
        for b in range(SPAN):
            half = upper if b < SPAN // 2 else lower
            cols = slice(b * BLK, (b + 1) * BLK)
            out[:, cols] = base[:, cols] + half[b % (SPAN // 2), 0].T

    @pl.when(jnp.logical_not(both))
    def _():
        out[...] = base[...]


def finish(meta, base, upper, lower):
    size = (SPAN * BLK, SPAN * BLK)
    rows = pl.BlockSpec((BLK, SPAN * BLK), lambda a, meta: (a, 0))
    tall = pl.BlockSpec((SPAN // 2, 1, BLK, BLK), lambda a, meta: (0, a, 0, 0))
    grid_spec = pltpu.PrefetchScalarGridSpec(
        num_scalar_prefetch=1, grid=(SPAN,), in_specs=[rows, tall, tall], out_specs=rows
    )
    return pl.pallas_call(
        finish_kernel,
        grid_spec=grid_spec,
        out_shape=jax.ShapeDtypeStruct(size, jnp.float32),
        name="finish",
    )(meta, base, upper, lower)


def swap_pairs(size, bit):
    return [(k, k ^ bit) for k in range(size)]


def spread(v, step):
    if step != "x":
        return v + lax.ppermute(v, step, [(0, 1)])
    v = v + lax.ppermute(v, "x", [(0, 1)]) + lax.ppermute(v, "x", [(0, 3)])
    return v + lax.ppermute(v, "x", [(1, 2)])


def body(border, row_scale, block_pick, given_diag):
    i = lax.axis_index(GR).astype(jnp.int32)
    j = lax.axis_index(GC).astype(jnp.int32)
    chip = i // 2
    core = i % 2
    meta = jnp.stack([chip, core, i, j])

    scaled = (jnp.sqrt(row_scale)[:, :, None] * border.astype(jnp.float32)).astype(jnp.bfloat16)

    own = jnp.einsum("srx,sry->sxy", scaled, scaled, preferred_element_type=jnp.float32)
    own_pick = lax.dynamic_slice(block_pick, (j * GROUP, i), (GROUP, 1))[:, 0]
    hot = own_pick[:, None] == jnp.arange(SPAN, dtype=jnp.int32)[None, :]
    diag = jnp.sum(jnp.where(hot[:, :, None, None], own[:, None], 0.0), axis=0)
    for bit in (1, 2, 4):
        diag = diag + lax.ppermute(diag, "z", swap_pairs(8, bit))

    peers = jnp.arange(8, dtype=jnp.int32)
    early = (peers < chip) | ((peers == chip) & (core == 1))
    slots = jnp.where(early[:, None, None, None], scaled[None, :HALF], scaled[None, HALF:])
    same = lax.all_to_all(slots, ("x", "yh"), 0, 0, tiled=True)
    cut = R // 2
    rootly = jnp.where(i == 0, scaled[:HALF], jnp.zeros_like(scaled[:HALF]))
    piece = rootly[:, :cut] + lax.ppermute(rootly[:, cut:], "core", [(0, 1)])
    flipped = flip(scaled)
    same, diag, piece, flipped = lax.optimization_barrier((same, diag, piece, flipped))

    other = lax.ppermute(same, "core", [(0, 1), (1, 0)])
    across = lax.ppermute(diag, "yl", swap_pairs(2, 1))
    tiles, late = gram_slots(meta, flipped, same, other)
    across, late = lax.optimization_barrier((across, late))
    diag = diag + across
    eye = jnp.eye(BLK, dtype=jnp.float32)
    given_here = lax.dynamic_slice(given_diag, (i * SPAN * BLK,), (SPAN * BLK,))
    diag = diag + given_here.reshape(SPAN, 1, BLK) * eye
    corner = spread(jnp.where(i == 0, diag, 0.0), "core")
    corner = spread(corner, "yh")
    piece = spread(piece, "yh")

    tiles = lax.all_to_all(tiles, GC, 0, 0, tiled=True)
    chol, inverse = factor(spread(corner, "x"))
    piece = spread(piece, "x")
    twin = lax.ppermute(piece, "core", [(0, 1), (1, 0)])
    lead = jnp.concatenate(
        [jnp.where(core == 0, piece, twin), jnp.where(core == 0, twin, piece)], axis=1
    )
    slices = panel_slots(scaled, lead, late)
    tiles, slices, chol, inverse = lax.optimization_barrier((tiles, slices, chol, inverse))

    upper, lower = place_tiles(meta, block_pick, tiles)
    slices = lax.all_to_all(slices, GC, 0, 0, tiled=True)
    everywhere = [(r * NWIN + c, c * NWIN + r) for r in range(NWIN) for c in range(NWIN)]
    strip = place_strip(meta, block_pick, slices)
    right = lax.ppermute(strip, AXES, everywhere)[None]
    copies = jnp.broadcast_to(strip, (NWIN,) + strip.shape)
    left = lax.all_to_all(copies, GC, 0, 0, tiled=True)
    inner = [
        (r * NWIN + c, c * NWIN + r) for r in range(1, NWIN) for c in range(1, NWIN) if r != c
    ]
    mirror_a = lax.ppermute(upper, AXES, inner)
    mirror_b = lax.ppermute(lower, AXES, inner)
    for axis, pairs in (
        ("yh", swap_pairs(2, 1)),
        ("x", swap_pairs(4, 1)),
        ("x", swap_pairs(4, 3)),
        ("core", swap_pairs(2, 1)),
    ):
        right = jnp.concatenate([right, lax.ppermute(right, axis, pairs)], axis=0)
    lefts, high, low = solve_rows(left, inverse)
    base = update(meta, upper, lower, lefts, high, low, right, diag, chol, inverse)
    return finish(meta, base, mirror_a, mirror_b)


def solution(mesh):
    fine = Mesh(np.asarray(mesh.devices).reshape(SIZES), AXES)
    in_specs = (P(GC, None, GR), P(GC, None), P(), P())
    return jax.shard_map(body, mesh=fine, in_specs=in_specs, out_specs=P(GR, GC), check_vma=False)
```
